32 devices in a mesh: fx: 8 (over z, x), fy: 4 (over y, core).
Axes of the slice: x: 2, y: 2, z: 4, core: 2. Of those that a mesh axis runs over, the one named last changes fastest.
Arguments:
- sky_image: float32 [16, 16384], P('fy', 'fx'), may hold values from -6 to 6
- col_off: int32 [8], replicated, may hold values from 0 to 16383
- row_off: int32 [4], replicated, may hold values from 0 to 65535
- layer_counts: int32 [8, 4], P('fx', 'fy'), may hold values from 1 to 8
- w_steps: int32 [8, 4, 8], P('fx', 'fy'), may hold values from 1 to 4
- live_blocks: int32 [8, 4], P('fx', 'fy'), may hold values from 1 to 16
- block_codes: int32 [8, 4, 16], P('fx', 'fy'), may hold values from 0 to 839
- vis_coords: float32 [8, 4, 16, 2, 128], P('fx', 'fy'), may hold values from 0 to 1
Outputs:
- visibilities: float32 [8, 4, 16, 2, 128], P('fx', 'fy')
The draws below stay inside these ranges and needn't reach their ends.
All inputs are finite; a program needn't handle non-finite values.
Results may differ from the reference program's by a relative error of at most 0.018.
Values may be sent and summed in bfloat16 or wider, within the bound.
No kernel may reach another device: no remote copies, remote signals or barrier semaphores. Data moves between devices by JAX's collectives and lax.ppermute only.
A program may use at most 64 MiB of HBM per device.

```python
import math
import jax
import jax.numpy as jnp
from jax import lax

FC = 2048
SG = 1024
NSKY = 65536
FR = 4
WL = 8
NB = 16
NV = 128
SG0 = 16
NSKY0 = 16
NSKY1 = 16384
N_FX = 8
N_FY = 4


def touch_ends(drawn, own_key, least, top_value):
    longest = drawn.shape.index(max(drawn.shape))
    spots = []
    for shift in (0, 1):
        where = [jax.random.randint(jax.random.fold_in(own_key, axis), (), 0, length) for axis, length in enumerate(drawn.shape)]
        where[longest] = (where[longest] + shift) % drawn.shape[longest]
        spots.append(tuple(where))
    return drawn.at[spots[0]].set(least).at[spots[1]].set(top_value)


def block_scale(own_key, extent, split, least, largest):
    def one(position, blocks):
        draws = jax.random.uniform(jax.random.fold_in(jax.random.fold_in(own_key, 6), position), (blocks,), jnp.float32, least / len(split), largest / len(split))
        return jnp.repeat(jnp.exp(draws), extent[position] // blocks).reshape((-1,) + (1,) * (len(extent) - position - 1))

    gain = one(*split[0])
    for cut in split[1:]:
        gain = gain * one(*cut)
    return gain


def normal_values(key, extent, scale, reach, cuts=(), kind=jnp.bfloat16):
    result = scale * jax.random.normal(key, extent, jnp.float32)
    if cuts:
        result = result * block_scale(key, extent, cuts, -0.22, 0.18)
    return jnp.clip(result, -reach, reach).astype(kind)


def setup_inputs(seed: int = 0) -> dict:
    arg_keys = jax.random.split(jax.random.key(seed), 9)
    sky_image = normal_values(arg_keys[0], (NSKY0, NSKY1), 1.0, 6.0, ((0, 4), (1, 8)), jnp.float32)
    col_off = touch_ends(jax.random.randint(arg_keys[1], (N_FX,), 0, NSKY1), jax.random.fold_in(arg_keys[1], 1), 0, NSKY1 - 1).astype(jnp.int32)
    row_off = touch_ends(jax.random.randint(arg_keys[2], (N_FY,), 0, NSKY), jax.random.fold_in(arg_keys[2], 1), 0, NSKY - 1).astype(jnp.int32)
    layer_counts = touch_ends(jax.random.randint(arg_keys[3], (N_FX, N_FY), 1, WL + 1), jax.random.fold_in(arg_keys[3], 1), 1, WL).astype(jnp.int32)
    w_steps = touch_ends(jax.random.randint(arg_keys[4], (N_FX, N_FY, WL), 1, 5), jax.random.fold_in(arg_keys[4], 1), 1, 4).astype(jnp.int32)
    live_blocks = touch_ends(jax.random.randint(arg_keys[5], (N_FX, N_FY), 1, NB + 1), jax.random.fold_in(arg_keys[5], 1), 1, NB).astype(jnp.int32)
    block_codes = touch_ends(jax.random.randint(arg_keys[6], (N_FX, N_FY, NB), 0, 840), jax.random.fold_in(arg_keys[6], 1), 0, 839).astype(jnp.int32)
    vis_coords = jnp.clip(1.0 * jax.random.uniform(arg_keys[7], (N_FX, N_FY, NB, 2, NV), jnp.float32) ** block_scale(arg_keys[7], (N_FX, N_FY, NB, 2, NV), ((0, 8), (1, 4)), -0.2, 0.2), 0.0, 1.0)
    return {"sky_image": sky_image, "col_off": col_off, "row_off": row_off, "layer_counts": layer_counts, "w_steps": w_steps, "live_blocks": live_blocks, "block_codes": block_codes, "vis_coords": vis_coords}


two_pi = 6.283185307179586
coarse_step = 32

def mulmod(factor_a, factor_b, modulus):
    high_part = factor_b // 256
    low_part = factor_b % 256
    reduced = factor_a * high_part % modulus
    return (reduced * 256 + factor_a * low_part) % modulus

def build_layers(subgrid, steps_list):
    rows_grid = subgrid.shape[0]
    cols_grid = subgrid.shape[1] // 2
    depths = jnp.cumsum(steps_list).astype(jnp.int32)
    centre_rows = jnp.arange(rows_grid, dtype=jnp.int32) - rows_grid // 2
    centre_cols = jnp.arange(cols_grid, dtype=jnp.int32) - cols_grid // 2
    radial = centre_rows[:, None] * centre_rows[:, None] + centre_cols[None, :] * centre_cols[None, :]
    screen = math.pi / cols_grid * (depths[:, None, None] * radial[None, :, :] % (2 * cols_grid)).astype(jnp.float32)
    cosine = jnp.cos(screen)
    sine_part = jnp.sin(screen)
    grid_real = subgrid[:, :cols_grid]
    grid_imag = subgrid[:, cols_grid:]
    layer_real = grid_real[None] * cosine - grid_imag[None] * sine_part
    layer_imag = grid_real[None] * sine_part + grid_imag[None] * cosine
    return jnp.concatenate([layer_real, layer_imag], axis=1).astype(jnp.bfloat16)

def kernel_visibilities(stacked, u_pos, v_pos):
    rows_grid = stacked.shape[0] // 2
    cols_grid = stacked.shape[1]
    count_vis = v_pos.shape[0]
    coarse = (jnp.arange(cols_grid // coarse_step, dtype=jnp.int32) * coarse_step).astype(jnp.float32)
    fine_part = jnp.arange(coarse_step, dtype=jnp.int32).astype(jnp.float32)
    coarse_angle = two_pi * coarse[:, None] * v_pos[None, :]
    fine_angle = two_pi * fine_part[:, None] * v_pos[None, :]
    coarse_cos = jnp.cos(coarse_angle)[:, None, :]
    coarse_sin = jnp.sin(coarse_angle)[:, None, :]
    fine_cos = jnp.cos(fine_angle)[None, :, :]
    fine_sin = jnp.sin(fine_angle)[None, :, :]
    kernel_real = (coarse_cos * fine_cos - coarse_sin * fine_sin).reshape(cols_grid, count_vis)
    kernel_imag = (coarse_sin * fine_cos + coarse_cos * fine_sin).reshape(cols_grid, count_vis)
    kernel = jnp.concatenate([kernel_real, kernel_imag], axis=1).astype(jnp.bfloat16)
    products = jnp.dot(stacked, kernel, preferred_element_type=jnp.float32)
    part_real = products[:rows_grid, :count_vis] - products[rows_grid:, count_vis:]
    part_imag = products[:rows_grid, count_vis:] + products[rows_grid:, :count_vis]
    row_angle = two_pi * jnp.arange(rows_grid, dtype=jnp.int32).astype(jnp.float32)[:, None] * u_pos[None, :]
    row_cos = jnp.cos(row_angle)
    row_sin = jnp.sin(row_angle)
    vis_scale = 1.0 / math.sqrt(rows_grid * cols_grid)
    vis_real = lax.optimization_barrier(jnp.sum(row_cos * part_real - row_sin * part_imag, axis=0)) * vis_scale
    vis_imag = lax.optimization_barrier(jnp.sum(row_cos * part_imag + row_sin * part_real, axis=0)) * vis_scale
    return jnp.stack([vis_real, vis_imag])

def reference(sky_image, col_off, row_off, layer_counts, w_steps, live_blocks, block_codes, vis_coords):
    total_cols = FC * N_FX
    total_rows = FR * N_FY
    band_cols = jnp.arange(SG, dtype=jnp.int32)
    wave_cols = ((col_off[:, None] + band_cols[None, :]) % total_cols).astype(jnp.int32)
    col_phase = -two_pi / total_cols
    col_scale = 1.0 / math.sqrt(total_cols)

    def add_facet(carry, facet_index):
        pieces = lax.dynamic_slice_in_dim(sky_image, facet_index * FC, FC, 1)
        spectrum = jnp.fft.fft(pieces, n=total_cols, axis=1)
        chosen = jnp.take(spectrum, wave_cols.reshape(-1), axis=1).reshape(total_rows, N_FX, SG)
        turned = mulmod(facet_index * FC % total_cols, wave_cols, total_cols)
        angles = col_phase * turned.astype(jnp.float32)
        post_cos = jnp.cos(angles)[None]
        post_sin = jnp.sin(angles)[None]
        real_part = jnp.real(chosen)
        imag_part = jnp.imag(chosen)
        band_real = (real_part * post_cos - imag_part * post_sin) * col_scale
        band_imag = (real_part * post_sin + imag_part * post_cos) * col_scale
        rounded = lax.optimization_barrier(jnp.stack([band_real, band_imag]).astype(jnp.bfloat16))
        return (carry + rounded.astype(jnp.float32), None)
    band_zero = jnp.zeros((2, total_rows, N_FX, SG), jnp.float32)
    band_total, unused = lax.scan(add_facet, band_zero, jnp.arange(N_FX, dtype=jnp.int32))
    strip_data = band_total.astype(jnp.bfloat16).astype(jnp.float32)
    row_phase = -two_pi / NSKY
    row_scale = 1.0 / math.sqrt(total_rows)
    wave_rows = ((row_off[:, None] + jnp.arange(SG0, dtype=jnp.int32)[None, :]) % NSKY).astype(jnp.int32)
    cell_rows = jnp.arange(total_rows, dtype=jnp.int32)
    sky_rows = (cell_rows // FR * (NSKY // N_FY) + cell_rows % FR).astype(jnp.int32)
    row_angles = row_phase * mulmod(sky_rows[None, None, :], wave_rows[:, :, None], NSKY).astype(jnp.float32)
    tab_cos = jnp.cos(row_angles)
    tab_sin = jnp.sin(row_angles)

    def contract(table_part, data_part):
        return jnp.einsum('rmx,xsj->srmj', table_part, data_part, precision=lax.Precision.HIGHEST)

    def add_row(carry, facet_row):
        data_real = lax.dynamic_slice_in_dim(strip_data[0], facet_row * FR, FR, 0)
        data_imag = lax.dynamic_slice_in_dim(strip_data[1], facet_row * FR, FR, 0)
        part_cos = lax.dynamic_slice_in_dim(tab_cos, facet_row * FR, FR, 2)
        part_sin = lax.dynamic_slice_in_dim(tab_sin, facet_row * FR, FR, 2)
        term_real = (contract(part_cos, data_real) - contract(part_sin, data_imag)) * row_scale
        term_imag = (contract(part_cos, data_imag) + contract(part_sin, data_real)) * row_scale
        rounded = lax.optimization_barrier(jnp.stack([term_real, term_imag], axis=2).astype(jnp.bfloat16))
        return (carry + rounded.astype(jnp.float32), None)
    grid_zero = jnp.zeros((N_FX, N_FY, 2, SG0, SG), jnp.float32)
    grids, unused_rows = lax.scan(add_row, grid_zero, jnp.arange(N_FY, dtype=jnp.int32))
    flat_grids = grids.reshape(N_FX * N_FY, 2, SG0, SG)

    def per_subgrid(packed):
        grid_pair, steps_list, count_here, live_here, codes_here, coords_here = packed
        subgrid = jnp.concatenate([grid_pair[0], grid_pair[1]], axis=1)
        layers = build_layers(subgrid, steps_list)

        def per_block(inputs):
            block_index, code_value, coords = inputs
            stacked = lax.dynamic_index_in_dim(layers, code_value % count_here, 0, keepdims=False)
            values = kernel_visibilities(stacked, coords[0], coords[1])
            return jnp.where(block_index < live_here, values, jnp.zeros_like(values))
        return lax.map(per_block, (jnp.arange(NB, dtype=jnp.int32), codes_here, coords_here))
    outputs = lax.map(per_subgrid, (flat_grids, w_steps.reshape(N_FX * N_FY, WL), layer_counts.reshape(-1), live_blocks.reshape(-1), block_codes.reshape(N_FX * N_FY, NB), vis_coords.reshape(N_FX * N_FY, NB, 2, NV)))
    return outputs.reshape(N_FX, N_FY, NB, 2, NV)
```

```python
import functools
import math

import jax
import jax.numpy as jnp
from jax import lax
from jax.experimental import pallas as pl
from jax.experimental.pallas import tpu as pltpu
from jax.sharding import PartitionSpec as P

SG = 1024
NSKY = 65536

LANES = 128
FINE = 16

COS_POLY = (
    0.9999999890590228,
    -19.73920449945383,
    64.93911745989081,
    -85.45013953079767,
    60.167630950263465,
    -25.967599245923743,
    6.52865815775625,
)
SIN_POLY = (
    6.283184916495428,
    -41.34158923268831,
    81.59994332977429,
    -76.61447253115396,
    41.34288235413569,
    -12.471243534350362,
)


def horner(coefficients, value):
    total = jnp.full_like(value, coefficients[-1])
    for coefficient in coefficients[-2::-1]:
        total = total * value + coefficient
    return total


def turn(fraction):
    square = fraction * fraction
    return horner(COS_POLY, square), fraction * horner(SIN_POLY, square)


def turn_of_int(count, modulus):
    half = modulus // 2
    centred = ((count + half) & (modulus - 1)) - half
    return turn(centred.astype(jnp.float32) * (1.0 / modulus))


def wrap(value):
    return value - jnp.round(value)


def iota(shape, axis):
    return lax.broadcasted_iota(jnp.int32, shape, axis)


def column_tables_kernel(dims, col_off, first, twiddle, second):
    half_z, facet_rows, fine_cols, total_cols, wide, scale = dims
    here = lax.axis_index("fx")
    for target in range(2):
        offset = col_off[here ^ target]
        residue = offset + iota((facet_rows, LANES), 1)
        for slot in range(half_z):
            row = facet_rows * (here ^ (2 * slot)) + iota((facet_rows, LANES), 0)
            cosine, sine = turn_of_int(row * residue, LANES)
            rows = pl.ds(slot * facet_rows, facet_rows)
            first[rows, pl.ds(target * LANES, LANES)] = cosine.astype(jnp.bfloat16)
            first[rows, pl.ds((2 + target) * LANES, LANES)] = (-sine).astype(jnp.bfloat16)
        phase = iota((fine_cols, LANES), 0) * (offset + iota((fine_cols, LANES), 1))
        cosine, sine = turn_of_int(phase, total_cols)
        cols = pl.ds(target * LANES, LANES)
        twiddle[0, :, cols] = cosine * scale
        twiddle[1, :, cols] = sine * (-scale)
    cosine, sine = turn_of_int(iota((wide, fine_cols), 0) * iota((wide, fine_cols), 1), fine_cols)
    second[pl.ds(0, wide), pl.ds(0, fine_cols)] = cosine.astype(jnp.bfloat16)
    second[pl.ds(0, wide), pl.ds(fine_cols, fine_cols)] = sine.astype(jnp.bfloat16)
    second[pl.ds(wide, wide), pl.ds(0, fine_cols)] = (-sine).astype(jnp.bfloat16)
    second[pl.ds(wide, wide), pl.ds(fine_cols, fine_cols)] = cosine.astype(jnp.bfloat16)


def band_kernel(dims, *refs):
    half_z, facet_rows, fine_cols, rows_here = dims
    pieces = refs[:half_z]
    first, twiddle, second, own_out, other_out = refs[half_z:]
    stacked = jnp.concatenate(
        [
            jnp.concatenate([piece[row] for piece in pieces], axis=0)
            for row in range(rows_here)
        ],
        axis=1,
    )
    spread = lax.dot_general(
        stacked, first[...], (((0,), (0,)), ((), ())), preferred_element_type=jnp.float32
    )
    twist_real = twiddle[0]
    twist_imag = twiddle[1]
    for row in range(rows_here):
        part = spread[row * fine_cols : (row + 1) * fine_cols]
        part_real = part[:, : 2 * LANES]
        part_imag = part[:, 2 * LANES :]
        turned = jnp.concatenate(
            [
                part_real * twist_real - part_imag * twist_imag,
                part_real * twist_imag + part_imag * twist_real,
            ],
            axis=0,
        ).astype(jnp.bfloat16)
        bands = jnp.dot(second[...], turned, preferred_element_type=jnp.float32)
        bands = bands.astype(jnp.bfloat16)
        own_out[row] = bands[:, :LANES]
        other_out[row] = bands[:, LANES:]


def vis_tables_kernel(
    dims, row_off, counts, steps, codes, coords, rows_out, cols_out, kernels, coarse_out, u_out
):
    half_y, rows_here, num_rows, rows_grid, cols_grid, blocks, row_scale, vis_scale = dims
    here = lax.axis_index("fy")
    taps = 4 * half_y * rows_here
    order = iota((rows_grid, taps), 1)
    imag_in = order & 1
    cell = (order // 2) % rows_here
    slot = order // (2 * rows_here)
    owner = here ^ (2 * (slot % half_y)) ^ (slot // half_y)
    sky_row = owner * (NSKY // num_rows) + cell
    wave = row_off[here] + iota((rows_grid, taps), 0)
    cosine, sine = turn_of_int(sky_row * (wave & (NSKY - 1)), NSKY)
    cosine = cosine * row_scale
    sine = sine * row_scale
    rows_out[pl.ds(0, rows_grid), :] = jnp.where(imag_in == 0, cosine, sine).astype(jnp.bfloat16)
    rows_out[pl.ds(rows_grid, rows_grid), :] = jnp.where(imag_in == 0, -sine, cosine).astype(
        jnp.bfloat16
    )
    layers = steps.shape[2]
    depths = []
    depth = steps[0, 0, 0]
    for layer in range(layers):
        if layer:
            depth = depth + steps[0, 0, layer]
        depths.append(depth)
    centre = iota((1, cols_grid), 1) - cols_grid // 2
    squares = centre * centre
    phases = jnp.concatenate([depth * squares for depth in depths], axis=0)
    cosine, sine = turn_of_int(phases, 2 * cols_grid)
    cols_out[0] = cosine
    cols_out[1] = sine
    coarse_count = cols_grid // LANES
    mids = LANES // FINE
    row_index = iota((rows_grid, LANES), 0)
    row_centre = row_index - rows_grid // 2
    row_squares = row_centre * row_centre
    for block in range(blocks):
        plane = lax.rem(codes[0, 0, block], counts[0, 0])
        depth = depths[0]
        for layer in range(1, layers):
            depth = jnp.where(plane >= layer, depths[layer], depth)
        u_pos = coords[0, 0, block, pl.ds(0, 1), :]
        v_pos = coords[0, 0, block, pl.ds(1, 1), :]
        half = cols_grid
        screen = ((depth * row_squares + half) & (2 * cols_grid - 1)) - half
        angle = wrap(row_index.astype(jnp.float32) * u_pos) + screen.astype(jnp.float32) * (
            1.0 / (2 * cols_grid)
        )
        cosine, sine = turn(wrap(angle))
        u_out[block, 0] = cosine * vis_scale
        u_out[block, 1] = sine * vis_scale
        steps_wide = iota((coarse_count, LANES), 0).astype(jnp.float32)
        cosine, sine = turn(wrap(steps_wide * wrap(v_pos * float(LANES))))
        coarse_out[block, 0] = cosine
        coarse_out[block, 1] = sine
        steps_mid = iota((mids, LANES), 0).astype(jnp.float32)
        mid_cos, mid_sin = turn(wrap(steps_mid * wrap(v_pos * float(FINE))))
        steps_fine = iota((FINE, LANES), 0).astype(jnp.float32)
        fine_cos, fine_sin = turn(wrap(steps_fine * v_pos))
        for mid in range(mids):
            head_cos = mid_cos[mid : mid + 1]
            head_sin = mid_sin[mid : mid + 1]
            real = (head_cos * fine_cos - head_sin * fine_sin).astype(jnp.bfloat16)
            imag = (head_sin * fine_cos + head_cos * fine_sin).astype(jnp.bfloat16)
            upper = pl.ds(mid * FINE, FINE)
            lower = pl.ds(LANES + mid * FINE, FINE)
            kernels[block, upper, pl.ds(0, LANES)] = real
            kernels[block, upper, pl.ds(LANES, LANES)] = imag
            kernels[block, lower, pl.ds(0, LANES)] = -imag
            kernels[block, lower, pl.ds(LANES, LANES)] = real


def degrid_kernel(
    dims, counts, live, codes, own, other, rows_tab, cols_tab, kernels, coarse, u_tab, out,
    strips, layers_ref,
):
    half_y, rows_here, rows_grid, cols_grid, blocks, layers = dims
    wide = cols_grid // LANES
    per_slot = rows_here * 2 * wide
    for slot in range(half_y):
        strips[pl.ds(slot * per_slot, per_slot), :] = (
            own[slot].astype(jnp.float32).reshape(per_slot, LANES)
        )
        strips[pl.ds((half_y + slot) * per_slot, per_slot), :] = (
            other[slot].astype(jnp.float32).reshape(per_slot, LANES)
        )
    taps = 4 * half_y * rows_here
    for part in range(wide):
        source = strips[pl.ds(part, taps, stride=wide), :].astype(jnp.bfloat16)
        grid = jnp.dot(rows_tab[...], source, preferred_element_type=jnp.float32)
        grid_real = grid[:rows_grid]
        grid_imag = grid[rows_grid:]
        cols = pl.ds(part * LANES, LANES)
        rows = pl.ds(part * rows_grid, rows_grid)
        for layer in range(layers):
            cosine = cols_tab[0, pl.ds(layer, 1), cols]
            sine = cols_tab[1, pl.ds(layer, 1), cols]
            layers_ref[layer, rows, pl.ds(0, LANES)] = (
                grid_real * cosine - grid_imag * sine
            ).astype(jnp.bfloat16)
            layers_ref[layer, rows, pl.ds(LANES, LANES)] = (
                grid_real * sine + grid_imag * cosine
            ).astype(jnp.bfloat16)
    for block in range(blocks):
        plane = lax.rem(codes[0, 0, block], counts[0, 0])
        sums = jnp.dot(layers_ref[plane], kernels[block], preferred_element_type=jnp.float32)
        total_real = jnp.zeros((rows_grid, LANES), jnp.float32)
        total_imag = jnp.zeros((rows_grid, LANES), jnp.float32)
        for part in range(wide):
            sum_real = sums[part * rows_grid : (part + 1) * rows_grid, :LANES]
            sum_imag = sums[part * rows_grid : (part + 1) * rows_grid, LANES:]
            cosine = coarse[block, 0, pl.ds(part, 1), :]
            sine = coarse[block, 1, pl.ds(part, 1), :]
            total_real = total_real + (sum_real * cosine - sum_imag * sine)
            total_imag = total_imag + (sum_real * sine + sum_imag * cosine)
        u_cos = u_tab[block, 0]
        u_sin = u_tab[block, 1]
        vis_real = jnp.sum(u_cos * total_real - u_sin * total_imag, axis=0, keepdims=True)
        vis_imag = jnp.sum(u_cos * total_imag + u_sin * total_real, axis=0, keepdims=True)
        keep = block < live[0, 0]
        out[0, 0, block, pl.ds(0, 1), :] = jnp.where(keep, vis_real, 0.0)
        out[0, 0, block, pl.ds(1, 1), :] = jnp.where(keep, vis_imag, 0.0)


def in_smem():
    return pl.BlockSpec(memory_space=pltpu.SMEM)


def in_vmem():
    return pl.BlockSpec(memory_space=pltpu.VMEM)


def per_device(
    sky_image, col_off, row_off, layer_counts, w_steps, live_blocks, block_codes, vis_coords
):
    rows_here, facet_cols = sky_image.shape
    num_cols = lax.axis_size("fx")
    num_rows = lax.axis_size("fy")
    half_z = num_cols // 2
    half_y = num_rows // 2
    total_cols = facet_cols * num_cols
    total_rows = rows_here * num_rows
    rows_grid = total_rows
    fine_cols = total_cols // LANES
    facet_rows = facet_cols // fine_cols
    wide = SG // LANES
    blocks = block_codes.shape[2]
    vis_count = vis_coords.shape[-1]
    layers = w_steps.shape[2]
    f32, bf16 = jnp.float32, jnp.bfloat16

    def exchange(value, flip):
        pairs = [(i, i ^ flip) for i in range(num_cols * num_rows)]
        return lax.ppermute(value, ("fx", "fy"), pairs)

    own_sky = sky_image.astype(bf16).reshape(rows_here, facet_rows, fine_cols)
    pieces = [own_sky]
    for slot in range(1, half_z):
        pieces.append(exchange(own_sky, 2 * slot * num_rows))

    first, twiddle, second = pl.pallas_call(
        functools.partial(
            column_tables_kernel,
            (half_z, facet_rows, fine_cols, total_cols, wide, 1.0 / math.sqrt(total_cols)),
        ),
        name="column_tables",
        out_shape=(
            jax.ShapeDtypeStruct((half_z * facet_rows, 4 * LANES), bf16),
            jax.ShapeDtypeStruct((2, fine_cols, 2 * LANES), f32),
            jax.ShapeDtypeStruct((2 * wide, 2 * fine_cols), bf16),
        ),
        in_specs=[in_smem()],
        out_specs=(in_vmem(),) * 3,
    )(col_off)

    taps = 2 * total_rows
    rows_tab, cols_tab, kernels, coarse, u_tab = pl.pallas_call(
        functools.partial(
            vis_tables_kernel,
            (
                half_y,
                rows_here,
                num_rows,
                rows_grid,
                SG,
                blocks,
                1.0 / math.sqrt(total_rows),
                1.0 / math.sqrt(rows_grid * SG),
            ),
        ),
        name="vis_tables",
        out_shape=(
            jax.ShapeDtypeStruct((2 * rows_grid, taps), bf16),
            jax.ShapeDtypeStruct((2, layers, SG), f32),
            jax.ShapeDtypeStruct((blocks, 2 * LANES, 2 * vis_count), bf16),
            jax.ShapeDtypeStruct((blocks, 2, wide, vis_count), f32),
            jax.ShapeDtypeStruct((blocks, 2, rows_grid, vis_count), f32),
        ),
        in_specs=[in_smem()] * 4 + [in_vmem()],
        out_specs=(in_vmem(),) * 5,
    )(row_off, layer_counts, w_steps, block_codes, vis_coords)

    band_shape = jax.ShapeDtypeStruct((rows_here, 2 * wide, LANES), bf16)
    own_band, other_band = pl.pallas_call(
        functools.partial(band_kernel, (half_z, facet_rows, fine_cols, rows_here)),
        name="bands",
        out_shape=(band_shape, band_shape),
        in_specs=[in_vmem()] * (half_z + 3),
        out_specs=(in_vmem(),) * 2,
    )(*pieces, first, twiddle, second)

    strips = []
    for slot in range(half_y):
        near = exchange(own_band, 2 * slot) if slot else own_band
        far = exchange(other_band, num_rows + 2 * slot)
        strips.append((near.astype(f32) + far.astype(f32)).astype(bf16))
    own_strips = jnp.stack(strips)
    other_strips = exchange(own_strips, 1)

    return pl.pallas_call(
        functools.partial(
            degrid_kernel, (half_y, rows_here, rows_grid, SG, blocks, layers)
        ),
        name="degrid",
        out_shape=jax.ShapeDtypeStruct(vis_coords.shape, f32),
        in_specs=[in_smem()] * 3 + [in_vmem()] * 7,
        out_specs=in_vmem(),
        scratch_shapes=[
            pltpu.VMEM((2 * half_y * rows_here * 2 * wide, LANES), f32),
            pltpu.VMEM((layers, wide * rows_grid, 2 * LANES), bf16),
        ],
    )(
        layer_counts, live_blocks, block_codes, own_strips, other_strips,
        rows_tab, cols_tab, kernels, coarse, u_tab,
    )


def solution(mesh):
    placed = (
        P("fy", "fx"),
        P(),
        P(),
        P("fx", "fy"),
        P("fx", "fy", None),
        P("fx", "fy"),
        P("fx", "fy", None),
        P("fx", "fy", None, None, None),
    )
    return jax.shard_map(
        per_device,
        mesh=mesh,
        in_specs=placed,
        out_specs=P("fx", "fy", None, None, None),
        check_vma=False,
    )
```

```python
import functools
import math

import jax
import jax.numpy as jnp
from jax import lax
from jax.experimental import pallas as pl
from jax.experimental.pallas import tpu as pltpu
from jax.sharding import PartitionSpec as P

SG = 1024
NSKY = 65536

LANES = 128
FINE = 16

COS_POLY = (
    0.9999999890590228,
    -19.73920449945383,
    64.93911745989081,
    -85.45013953079767,
    60.167630950263465,
    -25.967599245923743,
    6.52865815775625,
)
SIN_POLY = (
    6.283184916495428,
    -41.34158923268831,
    81.59994332977429,
    -76.61447253115396,
    41.34288235413569,
    -12.471243534350362,
)


def horner(coefficients, value):
    total = jnp.full_like(value, coefficients[-1])
    for coefficient in coefficients[-2::-1]:
        total = total * value + coefficient
    return total


def turn(fraction):
    square = fraction * fraction
    return horner(COS_POLY, square), fraction * horner(SIN_POLY, square)


def turn_of_int(count, modulus):
    half = modulus // 2
    centred = ((count + half) & (modulus - 1)) - half
    return turn(centred.astype(jnp.float32) * (1.0 / modulus))


def wrap(value):
    return value - jnp.round(value)


def iota(shape, axis):
    return lax.broadcasted_iota(jnp.int32, shape, axis)


def load_kernel(*refs):
    count = (len(refs) - 3) // 2
    sources, (sky_out, *targets) = refs[:count], refs[count : 2 * count]
    landed, split, semaphores = refs[2 * count :]
    copies = [
        pltpu.make_async_copy(source, target, semaphores.at[index])
        for index, (source, target) in enumerate(zip(sources, [landed, *targets]))
    ]
    for copy in copies:
        copy.start()
    copies[0].wait()
    rows, pieces, width = sky_out.shape
    parts = width // LANES
    for piece in range(pieces):
        for part in range(parts):
            split[pl.ds(part * rows * pieces + piece, rows, stride=pieces), :] = landed[
                :, pl.ds((piece * parts + part) * LANES, LANES)
            ]
    for row in range(rows):
        for part in range(parts):
            here = pl.ds((part * rows + row) * pieces, pieces)
            sky_out[row, :, pl.ds(part * LANES, LANES)] = split[here, :].astype(jnp.bfloat16)
    for copy in copies[1:]:
        copy.wait()


def column_tables_kernel(dims, col_off, first, twiddle, second):
    half_z, facet_rows, fine_cols, total_cols, wide, scale = dims
    here = lax.axis_index("fx")
    for target in range(2):
        offset = col_off[here ^ target]
        residue = offset + iota((facet_rows, LANES), 1)
        for slot in range(half_z):
            row = facet_rows * (here ^ (2 * slot)) + iota((facet_rows, LANES), 0)
            cosine, sine = turn_of_int(row * residue, LANES)
            rows = pl.ds(slot * facet_rows, facet_rows)
            first[rows, pl.ds(target * LANES, LANES)] = cosine.astype(jnp.bfloat16)
            first[rows, pl.ds((2 + target) * LANES, LANES)] = (-sine).astype(jnp.bfloat16)
        phase = iota((fine_cols, LANES), 0) * (offset + iota((fine_cols, LANES), 1))
        cosine, sine = turn_of_int(phase, total_cols)
        cols = pl.ds(target * LANES, LANES)
        twiddle[0, :, cols] = cosine * scale
        twiddle[1, :, cols] = sine * (-scale)
    cosine, sine = turn_of_int(iota((wide, fine_cols), 0) * iota((wide, fine_cols), 1), fine_cols)
    second[pl.ds(0, wide), pl.ds(0, fine_cols)] = cosine.astype(jnp.bfloat16)
    second[pl.ds(0, wide), pl.ds(fine_cols, fine_cols)] = sine.astype(jnp.bfloat16)
    second[pl.ds(wide, wide), pl.ds(0, fine_cols)] = (-sine).astype(jnp.bfloat16)
    second[pl.ds(wide, wide), pl.ds(fine_cols, fine_cols)] = cosine.astype(jnp.bfloat16)


def band_kernel(dims, *refs):
    half_z, facet_rows, fine_cols, rows_here = dims
    pieces = refs[:half_z]
    first, twiddle, second, own_out, other_out = refs[half_z:]
    stacked = jnp.concatenate(
        [
            jnp.concatenate([piece[row] for piece in pieces], axis=0)
            for row in range(rows_here)
        ],
        axis=1,
    )
    spread = lax.dot_general(
        stacked, first[...], (((0,), (0,)), ((), ())), preferred_element_type=jnp.float32
    )
    twist_real = twiddle[0]
    twist_imag = twiddle[1]
    for row in range(rows_here):
        part = spread[row * fine_cols : (row + 1) * fine_cols]
        part_real = part[:, : 2 * LANES]
        part_imag = part[:, 2 * LANES :]
        turned = jnp.concatenate(
            [
                part_real * twist_real - part_imag * twist_imag,
                part_real * twist_imag + part_imag * twist_real,
            ],
            axis=0,
        ).astype(jnp.bfloat16)
        bands = jnp.dot(second[...], turned, preferred_element_type=jnp.float32)
        bands = bands.astype(jnp.bfloat16)
        own_out[row] = bands[:, :LANES]
        other_out[row] = bands[:, LANES:]


def vis_tables_kernel(
    dims, row_off, steps, codes, limits_in, coords,
    rows_out, cols_out, kernels, coarse_out, u_out, planes, limits, semaphore,
):
    half_y, rows_here, num_rows, rows_grid, cols_grid, blocks, row_scale, vis_scale = dims
    here = lax.axis_index("fy")
    fetch = pltpu.make_async_copy(limits_in, limits, semaphore)
    fetch.start()
    taps = 4 * half_y * rows_here
    order = iota((rows_grid, taps), 1)
    imag_in = order & 1
    cell = (order // 2) % rows_here
    slot = order // (2 * rows_here)
    owner = here ^ (2 * (slot % half_y)) ^ (slot // half_y)
    sky_row = owner * (NSKY // num_rows) + cell
    wave = row_off[here] + iota((rows_grid, taps), 0)
    cosine, sine = turn_of_int(sky_row * (wave & (NSKY - 1)), NSKY)
    cosine = cosine * row_scale
    sine = sine * row_scale
    rows_out[pl.ds(0, rows_grid), :] = jnp.where(imag_in == 0, cosine, sine).astype(jnp.bfloat16)
    rows_out[pl.ds(rows_grid, rows_grid), :] = jnp.where(imag_in == 0, -sine, cosine).astype(
        jnp.bfloat16
    )
    layers = steps.shape[2]
    depths = []
    depth = steps[0, 0, 0]
    for layer in range(layers):
        if layer:
            depth = depth + steps[0, 0, layer]
        depths.append(depth)
    centre = iota((1, cols_grid), 1) - cols_grid // 2
    squares = centre * centre
    phases = jnp.concatenate([depth * squares for depth in depths], axis=0)
    cosine, sine = turn_of_int(phases, 2 * cols_grid)
    cols_out[0] = cosine
    cols_out[1] = sine
    fetch.wait()
    coarse_count = cols_grid // LANES
    mids = LANES // FINE
    row_index = iota((rows_grid, LANES), 0)
    row_centre = row_index - rows_grid // 2
    row_squares = row_centre * row_centre
    for block in range(blocks):
        plane = lax.rem(codes[0, 0, block], limits[0, 0])
        planes[block] = plane
        depth = depths[0]
        for layer in range(1, layers):
            depth = jnp.where(plane >= layer, depths[layer], depth)
        u_pos = coords[0, 0, block, pl.ds(0, 1), :]
        v_pos = coords[0, 0, block, pl.ds(1, 1), :]
        half = cols_grid
        screen = ((depth * row_squares + half) & (2 * cols_grid - 1)) - half
        angle = wrap(row_index.astype(jnp.float32) * u_pos) + screen.astype(jnp.float32) * (
            1.0 / (2 * cols_grid)
        )
        cosine, sine = turn(wrap(angle))
        weight = jnp.where(block < limits[0, 1], vis_scale, 0.0)
        u_out[block, 0] = cosine * weight
        u_out[block, 1] = sine * weight
        steps_wide = iota((coarse_count, LANES), 0).astype(jnp.float32)
        cosine, sine = turn(wrap(steps_wide * wrap(v_pos * float(LANES))))
        coarse_out[block, 0] = cosine
        coarse_out[block, 1] = sine
        steps_mid = iota((mids, LANES), 0).astype(jnp.float32)
        mid_cos, mid_sin = turn(wrap(steps_mid * wrap(v_pos * float(FINE))))
        steps_fine = iota((FINE, LANES), 0).astype(jnp.float32)
        fine_cos, fine_sin = turn(wrap(steps_fine * v_pos))
        for mid in range(mids):
            head_cos = mid_cos[mid : mid + 1]
            head_sin = mid_sin[mid : mid + 1]
            real = (head_cos * fine_cos - head_sin * fine_sin).astype(jnp.bfloat16)
            imag = (head_sin * fine_cos + head_cos * fine_sin).astype(jnp.bfloat16)
            upper = pl.ds(mid * FINE, FINE)
            lower = pl.ds(LANES + mid * FINE, FINE)
            kernels[block, upper, pl.ds(0, LANES)] = real
            kernels[block, upper, pl.ds(LANES, LANES)] = imag
            kernels[block, lower, pl.ds(0, LANES)] = -imag
            kernels[block, lower, pl.ds(LANES, LANES)] = real


def degrid_kernel(
    dims, planes, own, other, rows_tab, cols_tab, kernels, coarse, u_tab, out,
    strips, layers_ref,
):
    half_y, rows_here, rows_grid, cols_grid, blocks, layers = dims
    wide = cols_grid // LANES
    per_slot = rows_here * 2 * wide
    for slot in range(half_y):
        strips[pl.ds(slot * per_slot, per_slot), :] = (
            own[slot].astype(jnp.float32).reshape(per_slot, LANES)
        )
        strips[pl.ds((half_y + slot) * per_slot, per_slot), :] = (
            other[slot].astype(jnp.float32).reshape(per_slot, LANES)
        )
    taps = 4 * half_y * rows_here
    for part in range(wide):
        source = strips[pl.ds(part, taps, stride=wide), :].astype(jnp.bfloat16)
        grid = jnp.dot(rows_tab[...], source, preferred_element_type=jnp.float32)
        grid_real = grid[:rows_grid]
        grid_imag = grid[rows_grid:]
        cols = pl.ds(part * LANES, LANES)
        rows = pl.ds(part * rows_grid, rows_grid)
        for layer in range(layers):
            cosine = cols_tab[0, pl.ds(layer, 1), cols]
            sine = cols_tab[1, pl.ds(layer, 1), cols]
            layers_ref[layer, rows, pl.ds(0, LANES)] = (
                grid_real * cosine - grid_imag * sine
            ).astype(jnp.bfloat16)
            layers_ref[layer, rows, pl.ds(LANES, LANES)] = (
                grid_real * sine + grid_imag * cosine
            ).astype(jnp.bfloat16)
    for block in range(blocks):
        sums = jnp.dot(layers_ref[planes[block]], kernels[block], preferred_element_type=jnp.float32)
        total_real = jnp.zeros((rows_grid, LANES), jnp.float32)
        total_imag = jnp.zeros((rows_grid, LANES), jnp.float32)
        for part in range(wide):
            sum_real = sums[part * rows_grid : (part + 1) * rows_grid, :LANES]
            sum_imag = sums[part * rows_grid : (part + 1) * rows_grid, LANES:]
            cosine = coarse[block, 0, pl.ds(part, 1), :]
            sine = coarse[block, 1, pl.ds(part, 1), :]
            total_real = total_real + (sum_real * cosine - sum_imag * sine)
            total_imag = total_imag + (sum_real * sine + sum_imag * cosine)
        u_cos = u_tab[block, 0]
        u_sin = u_tab[block, 1]
        vis_real = jnp.sum(u_cos * total_real - u_sin * total_imag, axis=0, keepdims=True)
        vis_imag = jnp.sum(u_cos * total_imag + u_sin * total_real, axis=0, keepdims=True)
        out[0, 0, block, pl.ds(0, 1), :] = vis_real
        out[0, 0, block, pl.ds(1, 1), :] = vis_imag


def in_smem():
    return pl.BlockSpec(memory_space=pltpu.SMEM)


def in_vmem():
    return pl.BlockSpec(memory_space=pltpu.VMEM)


def kept(value):
    return pltpu.with_memory_space_constraint(value, pltpu.VMEM)


LIMIT = pltpu.CompilerParams(vmem_limit_bytes=16 << 20)


def per_device(
    sky_image, col_off, row_off, layer_counts, w_steps, live_blocks, block_codes, vis_coords
):
    rows_here, facet_cols = sky_image.shape
    num_cols = lax.axis_size("fx")
    num_rows = lax.axis_size("fy")
    half_z = num_cols // 2
    half_y = num_rows // 2
    total_cols = facet_cols * num_cols
    total_rows = rows_here * num_rows
    rows_grid = total_rows
    fine_cols = total_cols // LANES
    facet_rows = facet_cols // fine_cols
    wide = SG // LANES
    blocks = block_codes.shape[2]
    vis_count = vis_coords.shape[-1]
    layers = w_steps.shape[2]
    f32, bf16 = jnp.float32, jnp.bfloat16

    def exchange(value, flip):
        pairs = [(i, i ^ flip) for i in range(num_cols * num_rows)]
        return lax.ppermute(value, ("fx", "fy"), pairs)

    arguments = (
        sky_image, vis_coords, col_off, row_off, w_steps, block_codes
    )
    own_sky, coords, *scalars = pl.pallas_call(
        load_kernel,
        name="load",
        out_shape=(
            pltpu.VMEM((rows_here, facet_rows, fine_cols), bf16),
            pltpu.VMEM(vis_coords.shape, f32),
            *(pltpu.SMEM(value.shape, value.dtype) for value in arguments[2:]),
        ),
        in_specs=[pl.BlockSpec(memory_space=pl.ANY)] * len(arguments),
        out_specs=(in_vmem(),) * 2 + (in_smem(),) * (len(arguments) - 2),
        scratch_shapes=[
            pltpu.VMEM(sky_image.shape, f32),
            pltpu.VMEM((rows_here * facet_cols // LANES, LANES), f32),
            pltpu.SemaphoreType.DMA((len(arguments),)),
        ],
        compiler_params=LIMIT,
    )(*(pltpu.with_memory_space_constraint(value, pltpu.HBM) for value in arguments))
    coords = kept(coords)
    col_off, row_off, w_steps, block_codes = (
        pltpu.with_memory_space_constraint(value, pltpu.SMEM) for value in scalars
    )
    pieces = [own_sky]
    for slot in range(1, half_z):
        pieces.append(exchange(own_sky, 2 * slot * num_rows))

    first, twiddle, second = pl.pallas_call(
        functools.partial(
            column_tables_kernel,
            (half_z, facet_rows, fine_cols, total_cols, wide, 1.0 / math.sqrt(total_cols)),
        ),
        name="column_tables",
        out_shape=(
            pltpu.VMEM((half_z * facet_rows, 4 * LANES), bf16),
            pltpu.VMEM((2, fine_cols, 2 * LANES), f32),
            pltpu.VMEM((2 * wide, 2 * fine_cols), bf16),
        ),
        in_specs=[in_smem()],
        out_specs=(in_vmem(),) * 3,
        compiler_params=LIMIT,
    )(col_off)

    limits = jnp.where(
        lax.broadcasted_iota(jnp.int32, (1, LANES), 1) == 0, layer_counts, live_blocks
    )
    taps = 2 * total_rows
    *tables, planes = pl.pallas_call(
        functools.partial(
            vis_tables_kernel,
            (
                half_y,
                rows_here,
                num_rows,
                rows_grid,
                SG,
                blocks,
                1.0 / math.sqrt(total_rows),
                1.0 / math.sqrt(rows_grid * SG),
            ),
        ),
        name="vis_tables",
        out_shape=(
            pltpu.VMEM((2 * rows_grid, taps), bf16),
            pltpu.VMEM((2, layers, SG), f32),
            pltpu.VMEM((blocks, 2 * LANES, 2 * vis_count), bf16),
            pltpu.VMEM((blocks, 2, wide, vis_count), f32),
            pltpu.VMEM((blocks, 2, rows_grid, vis_count), f32),
            pltpu.SMEM((blocks,), jnp.int32),
        ),
        in_specs=[in_smem()] * 3 + [in_vmem()] * 2,
        out_specs=(in_vmem(),) * 5 + (in_smem(),),
        scratch_shapes=[pltpu.SMEM((1, LANES), jnp.int32), pltpu.SemaphoreType.DMA],
        compiler_params=LIMIT,
    )(row_off, w_steps, block_codes, kept(limits), coords)

    band_shape = pltpu.VMEM((rows_here, 2 * wide, LANES), bf16)
    own_band, other_band = pl.pallas_call(
        functools.partial(band_kernel, (half_z, facet_rows, fine_cols, rows_here)),
        name="bands",
        out_shape=(band_shape, band_shape),
        in_specs=[in_vmem()] * (half_z + 3),
        out_specs=(in_vmem(),) * 2,
        compiler_params=LIMIT,
    )(*(kept(value) for value in (*pieces, first, twiddle, second)))

    near, far = [own_band], []
    for slot in range(half_y):
        if slot:
            near.append(exchange(own_band, 2 * slot))
        far.append(exchange(other_band, num_rows + 2 * slot))
    near, far, tables = lax.optimization_barrier((near, far, tables))
    strips = [
        (one.astype(f32) + two.astype(f32)).astype(bf16) for one, two in zip(near, far)
    ]
    own_strips = jnp.stack(strips)
    other_strips = exchange(own_strips, 1)

    return pl.pallas_call(
        functools.partial(
            degrid_kernel, (half_y, rows_here, rows_grid, SG, blocks, layers)
        ),
        name="degrid",
        out_shape=jax.ShapeDtypeStruct(vis_coords.shape, f32),
        in_specs=[in_smem()] + [in_vmem()] * 7,
        out_specs=in_vmem(),
        scratch_shapes=[
            pltpu.VMEM((2 * half_y * rows_here * 2 * wide, LANES), f32),
            pltpu.VMEM((layers, wide * rows_grid, 2 * LANES), bf16),
        ],
        compiler_params=LIMIT,
    )(
        pltpu.with_memory_space_constraint(planes, pltpu.SMEM),
        *(kept(value) for value in (own_strips, other_strips, *tables)),
    )


def solution(mesh):
    placed = (
        P("fy", "fx"),
        P(),
        P(),
        P("fx", "fy"),
        P("fx", "fy", None),
        P("fx", "fy"),
        P("fx", "fy", None),
        P("fx", "fy", None, None, None),
    )
    return jax.shard_map(
        per_device,
        mesh=mesh,
        in_specs=placed,
        out_specs=P("fx", "fy", None, None, None),
        check_vma=False,
    )
```

```python
import functools
import math

import jax
import jax.numpy as jnp
from jax import lax
from jax.experimental import pallas as pl
from jax.experimental.pallas import tpu as pltpu
from jax.sharding import PartitionSpec as P

SG = 1024
NSKY = 65536

LANES = 128
FINE = 16

COS_POLY = (
    0.9999999890590228,
    -19.73920449945383,
    64.93911745989081,
    -85.45013953079767,
    60.167630950263465,
    -25.967599245923743,
    6.52865815775625,
)
SIN_POLY = (
    6.283184916495428,
    -41.34158923268831,
    81.59994332977429,
    -76.61447253115396,
    41.34288235413569,
    -12.471243534350362,
)


def horner(coefficients, value):
    total = jnp.full_like(value, coefficients[-1])
    for coefficient in coefficients[-2::-1]:
        total = total * value + coefficient
    return total


def turn(fraction):
    square = fraction * fraction
    return horner(COS_POLY, square), fraction * horner(SIN_POLY, square)


def turn_of_int(count, modulus):
    half = modulus // 2
    centred = ((count + half) & (modulus - 1)) - half
    return turn(centred.astype(jnp.float32) * (1.0 / modulus))


def wrap(value):
    return value - jnp.round(value)


def iota(shape, axis):
    return lax.broadcasted_iota(jnp.int32, shape, axis)


def load_kernel(*refs):
    count = (len(refs) - 3) // 2
    sources, (sky_out, *targets) = refs[:count], refs[count : 2 * count]
    landed, split, semaphores = refs[2 * count :]
    copies = [
        pltpu.make_async_copy(source, target, semaphores.at[index])
        for index, (source, target) in enumerate(zip(sources, [landed, *targets]))
    ]
    for copy in copies:
        copy.start()
    copies[0].wait()
    rows, pieces, width = sky_out.shape
    parts = width // LANES
    for piece in range(pieces):
        for part in range(parts):
            split[pl.ds(part * rows * pieces + piece, rows, stride=pieces), :] = landed[
                :, pl.ds((piece * parts + part) * LANES, LANES)
            ]
    for row in range(rows):
        for part in range(parts):
            here = pl.ds((part * rows + row) * pieces, pieces)
            sky_out[row, :, pl.ds(part * LANES, LANES)] = split[here, :].astype(jnp.bfloat16)
    for copy in copies[1:]:
        copy.wait()


def column_tables_kernel(dims, col_off, first, twiddle, second):
    half_z, facet_rows, fine_cols, total_cols, wide, scale = dims
    here = lax.axis_index("fx")
    for target in range(2):
        offset = col_off[here ^ target]
        residue = offset + iota((facet_rows, LANES), 1)
        for slot in range(half_z):
            row = facet_rows * (here ^ (2 * slot)) + iota((facet_rows, LANES), 0)
            cosine, sine = turn_of_int(row * residue, LANES)
            rows = pl.ds(slot * facet_rows, facet_rows)
            first[rows, pl.ds(target * LANES, LANES)] = cosine.astype(jnp.bfloat16)
            first[rows, pl.ds((2 + target) * LANES, LANES)] = (-sine).astype(jnp.bfloat16)
        phase = iota((fine_cols, LANES), 0) * (offset + iota((fine_cols, LANES), 1))
        cosine, sine = turn_of_int(phase, total_cols)
        cols = pl.ds(target * LANES, LANES)
        twiddle[0, :, cols] = cosine * scale
        twiddle[1, :, cols] = sine * (-scale)
    cosine, sine = turn_of_int(iota((wide, fine_cols), 0) * iota((wide, fine_cols), 1), fine_cols)
    second[pl.ds(0, wide), pl.ds(0, fine_cols)] = cosine.astype(jnp.bfloat16)
    second[pl.ds(0, wide), pl.ds(fine_cols, fine_cols)] = sine.astype(jnp.bfloat16)
    second[pl.ds(wide, wide), pl.ds(0, fine_cols)] = (-sine).astype(jnp.bfloat16)
    second[pl.ds(wide, wide), pl.ds(fine_cols, fine_cols)] = cosine.astype(jnp.bfloat16)


def band_kernel(dims, *refs):
    half_z, facet_rows, fine_cols, rows_here = dims
    pieces = refs[:half_z]
    first, twiddle, second, own_out, other_out = refs[half_z:]
    twist_real = twiddle[0]
    twist_imag = twiddle[1]
    for held in range(2):
        stacked = jnp.concatenate(
            [
                jnp.concatenate([piece[held, row] for piece in pieces], axis=0)
                for row in range(rows_here)
            ],
            axis=1,
        )
        spread = lax.dot_general(
            stacked, first[...], (((0,), (0,)), ((), ())), preferred_element_type=jnp.float32
        )
        for row in range(rows_here):
            part = spread[row * fine_cols : (row + 1) * fine_cols]
            part_real = part[:, : 2 * LANES]
            part_imag = part[:, 2 * LANES :]
            turned = jnp.concatenate(
                [
                    part_real * twist_real - part_imag * twist_imag,
                    part_real * twist_imag + part_imag * twist_real,
                ],
                axis=0,
            ).astype(jnp.bfloat16)
            bands = jnp.dot(second[...], turned, preferred_element_type=jnp.float32)
            bands = bands.astype(jnp.bfloat16)
            own_out[held, row] = bands[:, :LANES]
            other_out[held, row] = bands[:, LANES:]


def vis_tables_kernel(
    dims, row_off, steps, codes, limits_in, coords,
    cols_out, kernels, coarse_out, rows_out, planes, limits, u_tab, semaphore,
):
    half_y, rows_here, num_rows, rows_grid, cols_grid, blocks, row_scale, vis_scale = dims
    here = lax.axis_index("fy")
    fetch = pltpu.make_async_copy(limits_in, limits, semaphore)
    fetch.start()
    shape = (2 * rows_grid, 2 * rows_grid)
    order = iota(shape, 0)
    imag_out = order // rows_grid
    slot = (order // (2 * rows_here)) % half_y
    owner = ((here | 1) ^ (2 * slot)) - (order // rows_here) % 2
    sky_row = owner * (NSKY // num_rows) + order % rows_here
    column = iota(shape, 1)
    imag_in = column // rows_grid
    wave = row_off[here] + column % rows_grid
    cosine, sine = turn_of_int(sky_row * (wave & (NSKY - 1)), NSKY)
    cross = jnp.where(imag_out == 0, sine, -sine)
    row_weights = (jnp.where(imag_in == imag_out, cosine, cross) * row_scale).astype(jnp.bfloat16)
    layers = steps.shape[2]
    depths = []
    depth = steps[0, 0, 0]
    for layer in range(layers):
        if layer:
            depth = depth + steps[0, 0, layer]
        depths.append(depth)
    centre = iota((1, cols_grid), 1) - cols_grid // 2
    squares = centre * centre
    phases = jnp.concatenate([depth * squares for depth in depths], axis=0)
    cosine, sine = turn_of_int(phases, 2 * cols_grid)
    cols_out[0] = cosine
    cols_out[1] = sine
    fetch.wait()
    coarse_count = cols_grid // LANES
    mids = LANES // FINE
    row_index = iota((rows_grid, LANES), 0)
    row_centre = row_index - rows_grid // 2
    row_squares = row_centre * row_centre
    for block in range(blocks):
        plane = lax.rem(codes[0, 0, block], limits[0, 0])
        planes[block] = plane
        depth = depths[0]
        for layer in range(1, layers):
            depth = jnp.where(plane >= layer, depths[layer], depth)
        u_pos = coords[0, 0, block, pl.ds(0, 1), :]
        v_pos = coords[0, 0, block, pl.ds(1, 1), :]
        half = cols_grid
        screen = ((depth * row_squares + half) & (2 * cols_grid - 1)) - half
        angle = wrap(row_index.astype(jnp.float32) * u_pos) + screen.astype(jnp.float32) * (
            1.0 / (2 * cols_grid)
        )
        cosine, sine = turn(wrap(angle))
        weight = jnp.where(block < limits[0, 1], vis_scale, 0.0)
        spot = pl.ds(block * LANES, LANES)
        u_tab[pl.ds(0, rows_grid), spot] = (cosine * weight).astype(jnp.bfloat16)
        u_tab[pl.ds(rows_grid, rows_grid), spot] = (sine * weight).astype(jnp.bfloat16)
        steps_wide = iota((coarse_count, LANES), 0).astype(jnp.float32)
        cosine, sine = turn(wrap(steps_wide * wrap(v_pos * float(LANES))))
        coarse_out[block, 0] = cosine
        coarse_out[block, 1] = sine
        steps_mid = iota((mids, LANES), 0).astype(jnp.float32)
        mid_cos, mid_sin = turn(wrap(steps_mid * wrap(v_pos * float(FINE))))
        steps_fine = iota((FINE, LANES), 0).astype(jnp.float32)
        fine_cos, fine_sin = turn(wrap(steps_fine * v_pos))
        for mid in range(mids):
            head_cos = mid_cos[mid : mid + 1]
            head_sin = mid_sin[mid : mid + 1]
            real = (head_cos * fine_cos - head_sin * fine_sin).astype(jnp.bfloat16)
            imag = (head_sin * fine_cos + head_cos * fine_sin).astype(jnp.bfloat16)
            upper = pl.ds(mid * FINE, FINE)
            lower = pl.ds(LANES + mid * FINE, FINE)
            kernels[block, upper, pl.ds(0, LANES)] = real
            kernels[block, upper, pl.ds(LANES, LANES)] = imag
            kernels[block, lower, pl.ds(0, LANES)] = -imag
            kernels[block, lower, pl.ds(LANES, LANES)] = real
    weights = jnp.dot(row_weights, u_tab[...], preferred_element_type=jnp.float32)
    for block in range(blocks):
        for part in range(2):
            rows_out[block, part] = weights[
                part * rows_grid : (part + 1) * rows_grid, block * LANES : (block + 1) * LANES
            ]


def degrid_kernel(
    dims, planes, local, passed, cols_tab, kernels, coarse, rows_tab, out, strips, layers_ref
):
    held, cols_grid, blocks, layers = dims
    wide = cols_grid // LANES
    lead = lax.axis_index("fy") % 2 == 1
    size = 2 * wide
    for index in range(held):
        spot = (index // (local.shape[1] * local.shape[2]),
                index // local.shape[2] % local.shape[1], index % local.shape[2])
        strips[pl.ds(index * size, size), :] = jnp.where(
            lead, local[spot].astype(jnp.float32), passed[spot].astype(jnp.float32)
        )
    for part in range(0, wide, 2):
        pair = []
        for col in (part, part + 1):
            real = strips[pl.ds(col, held, stride=2 * wide), :]
            imag = strips[pl.ds(wide + col, held, stride=2 * wide), :]
            pair.append((col, real, imag))
        rows = pl.ds(part * held, 2 * held)
        for layer in range(layers):
            turned_real, turned_imag = [], []
            for col, real, imag in pair:
                cols = pl.ds(col * LANES, LANES)
                cosine = cols_tab[0, pl.ds(layer, 1), cols]
                sine = cols_tab[1, pl.ds(layer, 1), cols]
                turned_real.append(real * cosine - imag * sine)
                turned_imag.append(real * sine + imag * cosine)
            layers_ref[layer, rows, pl.ds(0, LANES)] = jnp.concatenate(turned_real).astype(
                jnp.bfloat16
            )
            layers_ref[layer, rows, pl.ds(LANES, LANES)] = jnp.concatenate(turned_imag).astype(
                jnp.bfloat16
            )
    for block in range(blocks):
        sums = jnp.dot(layers_ref[planes[block]], kernels[block], preferred_element_type=jnp.float32)
        total_real = jnp.zeros((held, LANES), jnp.float32)
        total_imag = jnp.zeros((held, LANES), jnp.float32)
        for part in range(wide):
            sum_real = sums[part * held : (part + 1) * held, :LANES]
            sum_imag = sums[part * held : (part + 1) * held, LANES:]
            cosine = coarse[block, 0, pl.ds(part, 1), :]
            sine = coarse[block, 1, pl.ds(part, 1), :]
            total_real = total_real + (sum_real * cosine - sum_imag * sine)
            total_imag = total_imag + (sum_real * sine + sum_imag * cosine)
        row_cos = rows_tab[block, 0]
        row_sin = rows_tab[block, 1]
        vis_real = jnp.sum(row_cos * total_real - row_sin * total_imag, axis=0, keepdims=True)
        vis_imag = jnp.sum(row_cos * total_imag + row_sin * total_real, axis=0, keepdims=True)
        for part, value in enumerate((vis_real, vis_imag)):
            spot = (0, 0, block, pl.ds(part, 1), slice(None))
            out[spot] = value


def in_smem():
    return pl.BlockSpec(memory_space=pltpu.SMEM)


def in_vmem():
    return pl.BlockSpec(memory_space=pltpu.VMEM)


def kept(value):
    return pltpu.with_memory_space_constraint(value, pltpu.VMEM)


LIMIT = pltpu.CompilerParams(vmem_limit_bytes=16 << 20)


def per_device(
    sky_image, col_off, row_off, layer_counts, w_steps, live_blocks, block_codes, vis_coords
):
    rows_here, facet_cols = sky_image.shape
    num_cols = lax.axis_size("fx")
    num_rows = lax.axis_size("fy")
    half_z = num_cols // 2
    half_y = num_rows // 2
    total_cols = facet_cols * num_cols
    total_rows = rows_here * num_rows
    rows_grid = total_rows
    fine_cols = total_cols // LANES
    facet_rows = facet_cols // fine_cols
    wide = SG // LANES
    blocks = block_codes.shape[2]
    vis_count = vis_coords.shape[-1]
    layers = w_steps.shape[2]
    f32, bf16 = jnp.float32, jnp.bfloat16

    def exchange(value, flip, other_flip):
        pairs = [
            (i, i ^ (flip if i % 2 else other_flip)) for i in range(num_cols * num_rows)
        ]
        return lax.ppermute(value, ("fx", "fy"), pairs)

    near_flip = 2 * num_rows
    arguments = (
        sky_image, vis_coords, col_off, row_off, w_steps, block_codes
    )
    own_sky, coords, *scalars = pl.pallas_call(
        load_kernel,
        name="load",
        out_shape=(
            pltpu.VMEM((rows_here, facet_rows, fine_cols), bf16),
            pltpu.VMEM(vis_coords.shape, f32),
            *(pltpu.SMEM(value.shape, value.dtype) for value in arguments[2:]),
        ),
        in_specs=[pl.BlockSpec(memory_space=pl.ANY)] * len(arguments),
        out_specs=(in_vmem(),) * 2 + (in_smem(),) * (len(arguments) - 2),
        scratch_shapes=[
            pltpu.VMEM(sky_image.shape, f32),
            pltpu.VMEM((rows_here * facet_cols // LANES, LANES), f32),
            pltpu.SemaphoreType.DMA((len(arguments),)),
        ],
        compiler_params=LIMIT,
    )(*(pltpu.with_memory_space_constraint(value, pltpu.HBM) for value in arguments))
    coords = kept(coords)
    col_off, row_off, w_steps, block_codes = (
        pltpu.with_memory_space_constraint(value, pltpu.SMEM) for value in scalars
    )
    chip_sky = jnp.stack([own_sky, exchange(own_sky, 1, 1)])
    pieces = [chip_sky]
    for slot in range(1, half_z):
        pieces.append(exchange(chip_sky, 2 * slot * num_rows, near_flip))

    first, twiddle, second = pl.pallas_call(
        functools.partial(
            column_tables_kernel,
            (half_z, facet_rows, fine_cols, total_cols, wide, 1.0 / math.sqrt(total_cols)),
        ),
        name="column_tables",
        out_shape=(
            pltpu.VMEM((half_z * facet_rows, 4 * LANES), bf16),
            pltpu.VMEM((2, fine_cols, 2 * LANES), f32),
            pltpu.VMEM((2 * wide, 2 * fine_cols), bf16),
        ),
        in_specs=[in_smem()],
        out_specs=(in_vmem(),) * 3,
        compiler_params=LIMIT,
    )(col_off)

    limits = jnp.where(
        lax.broadcasted_iota(jnp.int32, (1, LANES), 1) == 0, layer_counts, live_blocks
    )
    *tables, planes = pl.pallas_call(
        functools.partial(
            vis_tables_kernel,
            (
                half_y,
                rows_here,
                num_rows,
                rows_grid,
                SG,
                blocks,
                1.0 / math.sqrt(total_rows),
                1.0 / math.sqrt(rows_grid * SG),
            ),
        ),
        name="vis_tables",
        out_shape=(
            pltpu.VMEM((2, layers, SG), f32),
            pltpu.VMEM((blocks, 2 * LANES, 2 * vis_count), bf16),
            pltpu.VMEM((blocks, 2, wide, vis_count), f32),
            pltpu.VMEM((blocks, 2, rows_grid, vis_count), f32),
            pltpu.SMEM((blocks,), jnp.int32),
        ),
        in_specs=[in_smem()] * 3 + [in_vmem()] * 2,
        out_specs=(in_vmem(),) * 4 + (in_smem(),),
        scratch_shapes=[
            pltpu.SMEM((1, LANES), jnp.int32),
            pltpu.VMEM((2 * rows_grid, blocks * vis_count), bf16),
            pltpu.SemaphoreType.DMA,
        ],
        compiler_params=LIMIT,
    )(row_off, w_steps, block_codes, kept(limits), coords)

    band_shape = pltpu.VMEM((2, rows_here, 2 * wide, LANES), bf16)
    own_band, other_band = pl.pallas_call(
        functools.partial(band_kernel, (half_z, facet_rows, fine_cols, rows_here)),
        name="bands",
        out_shape=(band_shape, band_shape),
        in_specs=[in_vmem()] * (half_z + 3),
        out_specs=(in_vmem(),) * 2,
        compiler_params=LIMIT,
    )(*(kept(value) for value in (*pieces, first, twiddle, second)))

    near, far = [own_band], []
    for slot in range(half_y):
        if slot:
            near.append(exchange(own_band, 2 * slot, near_flip))
        far.append(exchange(other_band, num_rows + 2 * slot, near_flip))
    near, far, tables = lax.optimization_barrier((near, far, tables))
    strips = [
        (one.astype(f32) + two.astype(f32)).astype(bf16) for one, two in zip(near, far)
    ]
    own_strips = jnp.stack(strips)
    passed_strips = exchange(own_strips, 1, 1)

    operands = [kept(value) for value in (own_strips, passed_strips, *tables)]
    return pl.pallas_call(
        functools.partial(degrid_kernel, (total_rows, SG, blocks, layers)),
        name="degrid",
        out_shape=jax.ShapeDtypeStruct(vis_coords.shape, f32),
        in_specs=[in_smem()] + [in_vmem()] * len(operands),
        out_specs=in_vmem(),
        scratch_shapes=[
            pltpu.VMEM((total_rows * 2 * wide, LANES), f32),
            pltpu.VMEM((layers, wide * total_rows, 2 * LANES), bf16),
        ],
        compiler_params=LIMIT,
    )(pltpu.with_memory_space_constraint(planes, pltpu.SMEM), *operands)


def solution(mesh):
    placed = (
        P("fy", "fx"),
        P(),
        P(),
        P("fx", "fy"),
        P("fx", "fy", None),
        P("fx", "fy"),
        P("fx", "fy", None),
        P("fx", "fy", None, None, None),
    )
    return jax.shard_map(
        per_device,
        mesh=mesh,
        in_specs=placed,
        out_specs=P("fx", "fy", None, None, None),
        check_vma=False,
    )
```

```python
import functools
import math

import jax
import jax.numpy as jnp
from jax import lax
from jax.experimental import pallas as pl
from jax.experimental.pallas import tpu as pltpu
from jax.sharding import PartitionSpec as P

SG = 1024
NSKY = 65536

LANES = 128
FINE = 16

COS_POLY = (
    0.9999999890590228,
    -19.73920449945383,
    64.93911745989081,
    -85.45013953079767,
    60.167630950263465,
    -25.967599245923743,
    6.52865815775625,
)
SIN_POLY = (
    6.283184916495428,
    -41.34158923268831,
    81.59994332977429,
    -76.61447253115396,
    41.34288235413569,
    -12.471243534350362,
)


def horner(coefficients, value):
    total = jnp.full_like(value, coefficients[-1])
    for coefficient in coefficients[-2::-1]:
        total = total * value + coefficient
    return total


def turn(fraction):
    square = fraction * fraction
    return horner(COS_POLY, square), fraction * horner(SIN_POLY, square)


def turn_of_int(count, modulus):
    half = modulus // 2
    centred = ((count + half) & (modulus - 1)) - half
    return turn(centred.astype(jnp.float32) * (1.0 / modulus))


def wrap(value):
    return value - jnp.round(value)


def iota(shape, axis):
    return lax.broadcasted_iota(jnp.int32, shape, axis)


def settle(flat, split, target):
    rows, pieces, width = target.shape
    parts = width // LANES
    for piece in range(pieces):
        for part in range(parts):
            split[pl.ds(part * rows * pieces + piece, rows, stride=pieces), :] = flat[
                :, pl.ds((piece * parts + part) * LANES, LANES)
            ]
    for row in range(rows):
        for part in range(parts):
            here = pl.ds((part * rows + row) * pieces, pieces)
            target[row, :, pl.ds(part * LANES, LANES)] = split[here, :].astype(jnp.bfloat16)


def pack_kernel(own, passed, out, split):
    out[0] = own[...]
    settle(passed, split, out.at[1])


def load_kernel(*refs):
    count = (len(refs) - 3) // 2
    sources, (sky_out, *targets) = refs[:count], refs[count : 2 * count]
    landed, split, semaphores = refs[2 * count :]
    copies = [
        pltpu.make_async_copy(source, target, semaphores.at[index])
        for index, (source, target) in enumerate(zip(sources, [landed, *targets]))
    ]
    for copy in copies:
        copy.start()
    copies[0].wait()
    settle(landed, split, sky_out)
    for copy in copies[1:]:
        copy.wait()


def column_tables_kernel(dims, col_off, first, twiddle, second):
    half_z, facet_rows, fine_cols, total_cols, wide, scale = dims
    here = lax.axis_index("fx")
    for target in range(2):
        offset = col_off[here ^ target]
        residue = offset + iota((facet_rows, LANES), 1)
        for slot in range(half_z):
            row = facet_rows * (here ^ (2 * slot)) + iota((facet_rows, LANES), 0)
            cosine, sine = turn_of_int(row * residue, LANES)
            rows = pl.ds(slot * facet_rows, facet_rows)
            first[rows, pl.ds(target * LANES, LANES)] = cosine.astype(jnp.bfloat16)
            first[rows, pl.ds((2 + target) * LANES, LANES)] = (-sine).astype(jnp.bfloat16)
        phase = iota((fine_cols, LANES), 0) * (offset + iota((fine_cols, LANES), 1))
        cosine, sine = turn_of_int(phase, total_cols)
        cols = pl.ds(target * LANES, LANES)
        twiddle[0, :, cols] = cosine * scale
        twiddle[1, :, cols] = sine * (-scale)
    cosine, sine = turn_of_int(iota((wide, fine_cols), 0) * iota((wide, fine_cols), 1), fine_cols)
    second[pl.ds(0, wide), pl.ds(0, fine_cols)] = cosine.astype(jnp.bfloat16)
    second[pl.ds(0, wide), pl.ds(fine_cols, fine_cols)] = sine.astype(jnp.bfloat16)
    second[pl.ds(wide, wide), pl.ds(0, fine_cols)] = (-sine).astype(jnp.bfloat16)
    second[pl.ds(wide, wide), pl.ds(fine_cols, fine_cols)] = cosine.astype(jnp.bfloat16)


def band_kernel(dims, *refs):
    half_z, facet_rows, fine_cols, rows_here = dims
    pieces = refs[:half_z]
    first, twiddle, second, own_out, other_out = refs[half_z:]
    twist_real = twiddle[0]
    twist_imag = twiddle[1]
    for held in range(2):
        stacked = jnp.concatenate(
            [
                jnp.concatenate([piece[held, row] for piece in pieces], axis=0)
                for row in range(rows_here)
            ],
            axis=1,
        )
        spread = lax.dot_general(
            stacked, first[...], (((0,), (0,)), ((), ())), preferred_element_type=jnp.float32
        )
        for row in range(rows_here):
            part = spread[row * fine_cols : (row + 1) * fine_cols]
            part_real = part[:, : 2 * LANES]
            part_imag = part[:, 2 * LANES :]
            turned = jnp.concatenate(
                [
                    part_real * twist_real - part_imag * twist_imag,
                    part_real * twist_imag + part_imag * twist_real,
                ],
                axis=0,
            ).astype(jnp.bfloat16)
            bands = jnp.dot(second[...], turned, preferred_element_type=jnp.float32)
            bands = bands.astype(jnp.bfloat16)
            own_out[held, row] = bands[:, :LANES]
            other_out[held, row] = bands[:, LANES:]


def vis_tables_kernel(
    dims, row_off, steps, codes, limits_in, coords,
    cols_out, kernels, coarse_out, rows_out, planes, limits, u_tab, semaphore,
):
    half_y, rows_here, num_rows, rows_grid, cols_grid, blocks, row_scale, vis_scale = dims
    here = lax.axis_index("fy")
    fetch = pltpu.make_async_copy(limits_in, limits, semaphore)
    fetch.start()
    shape = (2 * rows_grid, 2 * rows_grid)
    order = iota(shape, 0)
    imag_out = order // rows_grid
    slot = (order // (2 * rows_here)) % half_y
    owner = ((here | 1) ^ (2 * slot)) - (order // rows_here) % 2
    sky_row = owner * (NSKY // num_rows) + order % rows_here
    column = iota(shape, 1)
    imag_in = column // rows_grid
    wave = row_off[here] + column % rows_grid
    cosine, sine = turn_of_int(sky_row * (wave & (NSKY - 1)), NSKY)
    cross = jnp.where(imag_out == 0, sine, -sine)
    row_weights = (jnp.where(imag_in == imag_out, cosine, cross) * row_scale).astype(jnp.bfloat16)
    layers = steps.shape[2]
    depths = []
    depth = steps[0, 0, 0]
    for layer in range(layers):
        if layer:
            depth = depth + steps[0, 0, layer]
        depths.append(depth)
    centre = iota((1, cols_grid), 1) - cols_grid // 2
    squares = centre * centre
    phases = jnp.concatenate([depth * squares for depth in depths], axis=0)
    cosine, sine = turn_of_int(phases, 2 * cols_grid)
    cols_out[0] = cosine
    cols_out[1] = sine
    fetch.wait()
    coarse_count = cols_grid // LANES
    mids = LANES // FINE
    row_index = iota((rows_grid, LANES), 0)
    row_centre = row_index - rows_grid // 2
    row_squares = row_centre * row_centre
    for block in range(blocks):
        plane = lax.rem(codes[0, 0, block], limits[0, 0])
        planes[block] = plane
        depth = depths[0]
        for layer in range(1, layers):
            depth = jnp.where(plane >= layer, depths[layer], depth)
        u_pos = coords[0, 0, block, pl.ds(0, 1), :]
        v_pos = coords[0, 0, block, pl.ds(1, 1), :]
        half = cols_grid
        screen = ((depth * row_squares + half) & (2 * cols_grid - 1)) - half
        angle = wrap(row_index.astype(jnp.float32) * u_pos) + screen.astype(jnp.float32) * (
            1.0 / (2 * cols_grid)
        )
        cosine, sine = turn(wrap(angle))
        weight = jnp.where(block < limits[0, 1], vis_scale, 0.0)
        spot = pl.ds(block * LANES, LANES)
        u_tab[pl.ds(0, rows_grid), spot] = (cosine * weight).astype(jnp.bfloat16)
        u_tab[pl.ds(rows_grid, rows_grid), spot] = (sine * weight).astype(jnp.bfloat16)
        steps_wide = iota((coarse_count, LANES), 0).astype(jnp.float32)
        cosine, sine = turn(wrap(steps_wide * wrap(v_pos * float(LANES))))
        coarse_out[block, 0] = cosine
        coarse_out[block, 1] = sine
        steps_mid = iota((mids, LANES), 0).astype(jnp.float32)
        mid_cos, mid_sin = turn(wrap(steps_mid * wrap(v_pos * float(FINE))))
        steps_fine = iota((FINE, LANES), 0).astype(jnp.float32)
        fine_cos, fine_sin = turn(wrap(steps_fine * v_pos))
        for mid in range(mids):
            head_cos = mid_cos[mid : mid + 1]
            head_sin = mid_sin[mid : mid + 1]
            real = (head_cos * fine_cos - head_sin * fine_sin).astype(jnp.bfloat16)
            imag = (head_sin * fine_cos + head_cos * fine_sin).astype(jnp.bfloat16)
            upper = pl.ds(mid * FINE, FINE)
            lower = pl.ds(LANES + mid * FINE, FINE)
            kernels[block, upper, pl.ds(0, LANES)] = real
            kernels[block, upper, pl.ds(LANES, LANES)] = imag
            kernels[block, lower, pl.ds(0, LANES)] = -imag
            kernels[block, lower, pl.ds(LANES, LANES)] = real
    weights = jnp.dot(row_weights, u_tab[...], preferred_element_type=jnp.float32)
    for block in range(blocks):
        for part in range(2):
            rows_out[block, part] = weights[
                part * rows_grid : (part + 1) * rows_grid, block * LANES : (block + 1) * LANES
            ]


def degrid_kernel(
    dims, planes, local, passed, cols_tab, kernels, coarse, rows_tab, out, strips, layers_ref
):
    held, cols_grid, blocks, layers = dims
    wide = cols_grid // LANES
    lead = lax.axis_index("fy") % 2 == 1
    size = 2 * wide
    for index in range(held):
        spot = (index // (local.shape[1] * local.shape[2]),
                index // local.shape[2] % local.shape[1], index % local.shape[2])
        strips[pl.ds(index * size, size), :] = jnp.where(
            lead, local[spot].astype(jnp.float32), passed[spot].astype(jnp.float32)
        )
    for part in range(0, wide, 2):
        pair = []
        for col in (part, part + 1):
            real = strips[pl.ds(col, held, stride=2 * wide), :]
            imag = strips[pl.ds(wide + col, held, stride=2 * wide), :]
            pair.append((col, real, imag))
        rows = pl.ds(part * held, 2 * held)
        for layer in range(layers):
            turned_real, turned_imag = [], []
            for col, real, imag in pair:
                cols = pl.ds(col * LANES, LANES)
                cosine = cols_tab[0, pl.ds(layer, 1), cols]
                sine = cols_tab[1, pl.ds(layer, 1), cols]
                turned_real.append(real * cosine - imag * sine)
                turned_imag.append(real * sine + imag * cosine)
            layers_ref[layer, rows, pl.ds(0, LANES)] = jnp.concatenate(turned_real).astype(
                jnp.bfloat16
            )
            layers_ref[layer, rows, pl.ds(LANES, LANES)] = jnp.concatenate(turned_imag).astype(
                jnp.bfloat16
            )
    for block in range(blocks):
        sums = jnp.dot(layers_ref[planes[block]], kernels[block], preferred_element_type=jnp.float32)
        total_real = jnp.zeros((held, LANES), jnp.float32)
        total_imag = jnp.zeros((held, LANES), jnp.float32)
        for part in range(wide):
            sum_real = sums[part * held : (part + 1) * held, :LANES]
            sum_imag = sums[part * held : (part + 1) * held, LANES:]
            cosine = coarse[block, 0, pl.ds(part, 1), :]
            sine = coarse[block, 1, pl.ds(part, 1), :]
            total_real = total_real + (sum_real * cosine - sum_imag * sine)
            total_imag = total_imag + (sum_real * sine + sum_imag * cosine)
        row_cos = rows_tab[block, 0]
        row_sin = rows_tab[block, 1]
        vis_real = jnp.sum(row_cos * total_real - row_sin * total_imag, axis=0, keepdims=True)
        vis_imag = jnp.sum(row_cos * total_imag + row_sin * total_real, axis=0, keepdims=True)
        for part, value in enumerate((vis_real, vis_imag)):
            spot = (0, 0, block, pl.ds(part, 1), slice(None))
            out[spot] = value


def in_smem():
    return pl.BlockSpec(memory_space=pltpu.SMEM)


def in_vmem():
    return pl.BlockSpec(memory_space=pltpu.VMEM)


def kept(value):
    return pltpu.with_memory_space_constraint(value, pltpu.VMEM)


LIMIT = pltpu.CompilerParams(vmem_limit_bytes=16 << 20)


def per_device(
    sky_image, col_off, row_off, layer_counts, w_steps, live_blocks, block_codes, vis_coords
):
    rows_here, facet_cols = sky_image.shape
    num_cols = lax.axis_size("fx")
    num_rows = lax.axis_size("fy")
    half_z = num_cols // 2
    half_y = num_rows // 2
    total_cols = facet_cols * num_cols
    total_rows = rows_here * num_rows
    rows_grid = total_rows
    fine_cols = total_cols // LANES
    facet_rows = facet_cols // fine_cols
    wide = SG // LANES
    blocks = block_codes.shape[2]
    vis_count = vis_coords.shape[-1]
    layers = w_steps.shape[2]
    f32, bf16 = jnp.float32, jnp.bfloat16

    def exchange(value, flip, other_flip):
        pairs = [
            (i, i ^ (flip if i % 2 else other_flip)) for i in range(num_cols * num_rows)
        ]
        return lax.ppermute(value, ("fx", "fy"), pairs)

    near_flip = 2 * num_rows
    passed_sky = exchange(sky_image, 1, 1)
    arguments = (
        sky_image, vis_coords, col_off, row_off, w_steps, block_codes
    )
    own_sky, coords, *scalars = pl.pallas_call(
        load_kernel,
        name="load",
        out_shape=(
            pltpu.VMEM((rows_here, facet_rows, fine_cols), bf16),
            pltpu.VMEM(vis_coords.shape, f32),
            *(pltpu.SMEM(value.shape, value.dtype) for value in arguments[2:]),
        ),
        in_specs=[pl.BlockSpec(memory_space=pl.ANY)] * len(arguments),
        out_specs=(in_vmem(),) * 2 + (in_smem(),) * (len(arguments) - 2),
        scratch_shapes=[
            pltpu.VMEM(sky_image.shape, f32),
            pltpu.VMEM((rows_here * facet_cols // LANES, LANES), f32),
            pltpu.SemaphoreType.DMA((len(arguments),)),
        ],
        compiler_params=LIMIT,
    )(*(pltpu.with_memory_space_constraint(value, pltpu.HBM) for value in arguments))
    coords = kept(coords)
    col_off, row_off, w_steps, block_codes = (
        pltpu.with_memory_space_constraint(value, pltpu.SMEM) for value in scalars
    )
    chip_sky = pl.pallas_call(
        pack_kernel,
        name="pack",
        out_shape=pltpu.VMEM((2, rows_here, facet_rows, fine_cols), bf16),
        in_specs=[in_vmem()] * 2,
        out_specs=in_vmem(),
        scratch_shapes=[pltpu.VMEM((rows_here * facet_cols // LANES, LANES), f32)],
        compiler_params=LIMIT,
    )(kept(own_sky), kept(passed_sky))
    pieces = [chip_sky]
    for slot in range(1, half_z):
        pieces.append(exchange(chip_sky, 2 * slot * num_rows, near_flip))

    first, twiddle, second = pl.pallas_call(
        functools.partial(
            column_tables_kernel,
            (half_z, facet_rows, fine_cols, total_cols, wide, 1.0 / math.sqrt(total_cols)),
        ),
        name="column_tables",
        out_shape=(
            pltpu.VMEM((half_z * facet_rows, 4 * LANES), bf16),
            pltpu.VMEM((2, fine_cols, 2 * LANES), f32),
            pltpu.VMEM((2 * wide, 2 * fine_cols), bf16),
        ),
        in_specs=[in_smem()],
        out_specs=(in_vmem(),) * 3,
        compiler_params=LIMIT,
    )(col_off)

    limits = jnp.where(
        lax.broadcasted_iota(jnp.int32, (1, LANES), 1) == 0, layer_counts, live_blocks
    )
    *tables, planes = pl.pallas_call(
        functools.partial(
            vis_tables_kernel,
            (
                half_y,
                rows_here,
                num_rows,
                rows_grid,
                SG,
                blocks,
                1.0 / math.sqrt(total_rows),
                1.0 / math.sqrt(rows_grid * SG),
            ),
        ),
        name="vis_tables",
        out_shape=(
            pltpu.VMEM((2, layers, SG), f32),
            pltpu.VMEM((blocks, 2 * LANES, 2 * vis_count), bf16),
            pltpu.VMEM((blocks, 2, wide, vis_count), f32),
            pltpu.VMEM((blocks, 2, rows_grid, vis_count), f32),
            pltpu.SMEM((blocks,), jnp.int32),
        ),
        in_specs=[in_smem()] * 3 + [in_vmem()] * 2,
        out_specs=(in_vmem(),) * 4 + (in_smem(),),
        scratch_shapes=[
            pltpu.SMEM((1, LANES), jnp.int32),
            pltpu.VMEM((2 * rows_grid, blocks * vis_count), bf16),
            pltpu.SemaphoreType.DMA,
        ],
        compiler_params=LIMIT,
    )(row_off, w_steps, block_codes, kept(limits), coords)

    band_shape = pltpu.VMEM((2, rows_here, 2 * wide, LANES), bf16)
    own_band, other_band = pl.pallas_call(
        functools.partial(band_kernel, (half_z, facet_rows, fine_cols, rows_here)),
        name="bands",
        out_shape=(band_shape, band_shape),
        in_specs=[in_vmem()] * (half_z + 3),
        out_specs=(in_vmem(),) * 2,
        compiler_params=LIMIT,
    )(*(kept(value) for value in (*pieces, first, twiddle, second)))

    near, far = [own_band], []
    for slot in range(half_y):
        if slot:
            near.append(exchange(own_band, 2 * slot, near_flip))
        far.append(exchange(other_band, num_rows + 2 * slot, near_flip))
    near, far, tables = lax.optimization_barrier((near, far, tables))
    strips = [
        (one.astype(f32) + two.astype(f32)).astype(bf16) for one, two in zip(near, far)
    ]
    own_strips = jnp.stack(strips)
    passed_strips = exchange(own_strips, 1, 1)

    operands = [kept(value) for value in (own_strips, passed_strips, *tables)]
    return pl.pallas_call(
        functools.partial(degrid_kernel, (total_rows, SG, blocks, layers)),
        name="degrid",
        out_shape=jax.ShapeDtypeStruct(vis_coords.shape, f32),
        in_specs=[in_smem()] + [in_vmem()] * len(operands),
        out_specs=in_vmem(),
        scratch_shapes=[
            pltpu.VMEM((total_rows * 2 * wide, LANES), f32),
            pltpu.VMEM((layers, wide * total_rows, 2 * LANES), bf16),
        ],
        compiler_params=LIMIT,
    )(pltpu.with_memory_space_constraint(planes, pltpu.SMEM), *operands)


def solution(mesh):
    placed = (
        P("fy", "fx"),
        P(),
        P(),
        P("fx", "fy"),
        P("fx", "fy", None),
        P("fx", "fy"),
        P("fx", "fy", None),
        P("fx", "fy", None, None, None),
    )
    return jax.shard_map(
        per_device,
        mesh=mesh,
        in_specs=placed,
        out_specs=P("fx", "fy", None, None, None),
        check_vma=False,
    )
```

```python
import functools
import math

import jax
import jax.numpy as jnp
from jax import lax
from jax.experimental import pallas as pl
from jax.experimental.pallas import tpu as pltpu
from jax.sharding import PartitionSpec as P

SG = 1024
NSKY = 65536

LANES = 128
FINE = 16

COS_POLY = (
    0.9999999890590228,
    -19.73920449945383,
    64.93911745989081,
    -85.45013953079767,
    60.167630950263465,
    -25.967599245923743,
    6.52865815775625,
)
SIN_POLY = (
    6.283184916495428,
    -41.34158923268831,
    81.59994332977429,
    -76.61447253115396,
    41.34288235413569,
    -12.471243534350362,
)


def horner(coefficients, value):
    total = jnp.full_like(value, coefficients[-1])
    for coefficient in coefficients[-2::-1]:
        total = total * value + coefficient
    return total


def turn(fraction):
    square = fraction * fraction
    return horner(COS_POLY, square), fraction * horner(SIN_POLY, square)


def turn_of_int(count, modulus):
    half = modulus // 2
    centred = ((count + half) & (modulus - 1)) - half
    return turn(centred.astype(jnp.float32) * (1.0 / modulus))


def wrap(value):
    return value - jnp.round(value)


def iota(shape, axis):
    return lax.broadcasted_iota(jnp.int32, shape, axis)


def settle(flat, split, target):
    rows, pieces, width = target.shape
    parts = width // LANES
    for piece in range(pieces):
        for part in range(parts):
            split[pl.ds(part * rows * pieces + piece, rows, stride=pieces), :] = flat[
                :, pl.ds((piece * parts + part) * LANES, LANES)
            ]
    for row in range(rows):
        for part in range(parts):
            here = pl.ds((part * rows + row) * pieces, pieces)
            target[row, :, pl.ds(part * LANES, LANES)] = split[here, :].astype(jnp.bfloat16)


def pack_kernel(own, passed, out, split):
    out[0] = own[...]
    settle(passed, split, out.at[1])


def load_kernel(*refs):
    count = (len(refs) - 3) // 2
    sources, (sky_out, *targets) = refs[:count], refs[count : 2 * count]
    landed, split, semaphores = refs[2 * count :]
    copies = [
        pltpu.make_async_copy(source, target, semaphores.at[index])
        for index, (source, target) in enumerate(zip(sources, [landed, *targets]))
    ]
    for copy in copies:
        copy.start()
    copies[0].wait()
    settle(landed, split, sky_out)
    for copy in copies[1:]:
        copy.wait()


def column_tables_kernel(dims, col_off, first, twiddle, second):
    half_z, facet_rows, fine_cols, total_cols, wide, scale = dims
    here = lax.axis_index("fx")
    for slot in range(half_z):
        row = facet_rows * (here ^ (2 * slot)) + iota((facet_rows, LANES), 0)
        cosine, sine = turn_of_int(row * iota((facet_rows, LANES), 1), LANES)
        rows = pl.ds(slot * facet_rows, facet_rows)
        first[rows, pl.ds(0, LANES)] = cosine.astype(jnp.bfloat16)
        first[rows, pl.ds(LANES, LANES)] = (-sine).astype(jnp.bfloat16)
    for target in range(2):
        offset = col_off[here ^ target]
        residue = iota((fine_cols, LANES), 1)
        step = (residue - offset) & (LANES - 1)
        cosine, sine = turn_of_int(iota((fine_cols, LANES), 0) * (offset + step), total_cols)
        cols = pl.ds(target * LANES, LANES)
        twiddle[0, :, cols] = cosine * scale
        twiddle[1, :, cols] = sine * (-scale)
    cosine, sine = turn_of_int(iota((wide, fine_cols), 0) * iota((wide, fine_cols), 1), fine_cols)
    second[pl.ds(0, wide), pl.ds(0, fine_cols)] = cosine.astype(jnp.bfloat16)
    second[pl.ds(0, wide), pl.ds(fine_cols, fine_cols)] = sine.astype(jnp.bfloat16)
    second[pl.ds(wide, wide), pl.ds(0, fine_cols)] = (-sine).astype(jnp.bfloat16)
    second[pl.ds(wide, wide), pl.ds(fine_cols, fine_cols)] = cosine.astype(jnp.bfloat16)


def band_kernel(dims, col_off, *refs):
    half_z, facet_rows, fine_cols, rows_here = dims
    here = lax.axis_index("fx")
    shifts = [(-col_off[here ^ target]) & (LANES - 1) for target in range(2)]
    pieces = refs[:half_z]
    first, twiddle, second, own_out, other_out = refs[half_z:]
    twist_real = twiddle[0]
    twist_imag = twiddle[1]
    for held in range(2):
        stacked = jnp.concatenate(
            [
                jnp.concatenate([piece[held, row] for piece in pieces], axis=0)
                for row in range(rows_here)
            ],
            axis=1,
        )
        spread = lax.dot_general(
            stacked, first[...], (((0,), (0,)), ((), ())), preferred_element_type=jnp.float32
        )
        for row in range(rows_here):
            part = spread[row * fine_cols : (row + 1) * fine_cols]
            part_real = jnp.concatenate([part[:, :LANES]] * 2, axis=1)
            part_imag = jnp.concatenate([part[:, LANES:]] * 2, axis=1)
            turned = jnp.concatenate(
                [
                    part_real * twist_real - part_imag * twist_imag,
                    part_real * twist_imag + part_imag * twist_real,
                ],
                axis=0,
            ).astype(jnp.bfloat16)
            bands = jnp.dot(second[...], turned, preferred_element_type=jnp.float32)
            for target, out in enumerate((own_out, other_out)):
                band = bands[:, target * LANES : (target + 1) * LANES]
                out[held, row] = pltpu.roll(band, shifts[target], 1).astype(jnp.bfloat16)


def vis_tables_kernel(
    dims, row_off, steps, codes, limits_in, coords,
    cols_out, kernels, coarse_out, rows_out, planes, limits, u_tab, semaphore,
):
    half_y, rows_here, num_rows, rows_grid, cols_grid, blocks, row_scale, vis_scale = dims
    here = lax.axis_index("fy")
    fetch = pltpu.make_async_copy(limits_in, limits, semaphore)
    fetch.start()
    shape = (2 * rows_grid, 2 * rows_grid)
    order = iota(shape, 0)
    imag_out = order // rows_grid
    slot = (order // (2 * rows_here)) % half_y
    owner = ((here | 1) ^ (2 * slot)) - (order // rows_here) % 2
    sky_row = owner * (NSKY // num_rows) + order % rows_here
    column = iota(shape, 1)
    imag_in = column // rows_grid
    wave = row_off[here] + column % rows_grid
    cosine, sine = turn_of_int(sky_row * (wave & (NSKY - 1)), NSKY)
    cross = jnp.where(imag_out == 0, sine, -sine)
    row_weights = (jnp.where(imag_in == imag_out, cosine, cross) * row_scale).astype(jnp.bfloat16)
    layers = steps.shape[2]
    depths = []
    depth = steps[0, 0, 0]
    for layer in range(layers):
        if layer:
            depth = depth + steps[0, 0, layer]
        depths.append(depth)
    centre = iota((1, cols_grid), 1) - cols_grid // 2
    squares = centre * centre
    phases = jnp.concatenate([depth * squares for depth in depths], axis=0)
    cosine, sine = turn_of_int(phases, 2 * cols_grid)
    cols_out[0] = cosine
    cols_out[1] = sine
    fetch.wait()
    coarse_count = cols_grid // LANES
    mids = LANES // FINE
    row_index = iota((rows_grid, LANES), 0)
    row_centre = row_index - rows_grid // 2
    row_squares = row_centre * row_centre
    for block in range(blocks):
        plane = lax.rem(codes[0, 0, block], limits[0, 0])
        planes[block] = plane
        depth = depths[0]
        for layer in range(1, layers):
            depth = jnp.where(plane >= layer, depths[layer], depth)
        u_pos = coords[0, 0, block, pl.ds(0, 1), :]
        v_pos = coords[0, 0, block, pl.ds(1, 1), :]
        half = cols_grid
        screen = ((depth * row_squares + half) & (2 * cols_grid - 1)) - half
        angle = wrap(row_index.astype(jnp.float32) * u_pos) + screen.astype(jnp.float32) * (
            1.0 / (2 * cols_grid)
        )
        cosine, sine = turn(wrap(angle))
        weight = jnp.where(block < limits[0, 1], vis_scale, 0.0)
        spot = pl.ds(block * LANES, LANES)
        u_tab[pl.ds(0, rows_grid), spot] = (cosine * weight).astype(jnp.bfloat16)
        u_tab[pl.ds(rows_grid, rows_grid), spot] = (sine * weight).astype(jnp.bfloat16)
        steps_wide = iota((coarse_count, LANES), 0).astype(jnp.float32)
        cosine, sine = turn(wrap(steps_wide * wrap(v_pos * float(LANES))))
        coarse_out[block, 0] = cosine
        coarse_out[block, 1] = sine
        steps_mid = iota((mids, LANES), 0).astype(jnp.float32)
        mid_cos, mid_sin = turn(wrap(steps_mid * wrap(v_pos * float(FINE))))
        steps_fine = iota((FINE, LANES), 0).astype(jnp.float32)
        fine_cos, fine_sin = turn(wrap(steps_fine * v_pos))
        for mid in range(mids):
            head_cos = mid_cos[mid : mid + 1]
            head_sin = mid_sin[mid : mid + 1]
            real = (head_cos * fine_cos - head_sin * fine_sin).astype(jnp.bfloat16)
            imag = (head_sin * fine_cos + head_cos * fine_sin).astype(jnp.bfloat16)
            upper = pl.ds(mid * FINE, FINE)
            lower = pl.ds(LANES + mid * FINE, FINE)
            kernels[block, upper, pl.ds(0, LANES)] = real
            kernels[block, upper, pl.ds(LANES, LANES)] = imag
            kernels[block, lower, pl.ds(0, LANES)] = -imag
            kernels[block, lower, pl.ds(LANES, LANES)] = real
    weights = jnp.dot(row_weights, u_tab[...], preferred_element_type=jnp.float32)
    for block in range(blocks):
        for part in range(2):
            rows_out[block, part] = weights[
                part * rows_grid : (part + 1) * rows_grid, block * LANES : (block + 1) * LANES
            ]


def degrid_kernel(
    dims, planes, local, passed, cols_tab, kernels, coarse, rows_tab, out, strips, layers_ref
):
    held, cols_grid, blocks, layers = dims
    wide = cols_grid // LANES
    lead = lax.axis_index("fy") % 2 == 1
    size = 2 * wide
    for index in range(held):
        spot = (index // (local.shape[1] * local.shape[2]),
                index // local.shape[2] % local.shape[1], index % local.shape[2])
        strips[pl.ds(index * size, size), :] = jnp.where(
            lead, local[spot].astype(jnp.float32), passed[spot].astype(jnp.float32)
        )
    for part in range(0, wide, 2):
        pair = []
        for col in (part, part + 1):
            real = strips[pl.ds(col, held, stride=2 * wide), :]
            imag = strips[pl.ds(wide + col, held, stride=2 * wide), :]
            pair.append((col, real, imag))
        rows = pl.ds(part * held, 2 * held)
        for layer in range(layers):
            turned_real, turned_imag = [], []
            for col, real, imag in pair:
                cols = pl.ds(col * LANES, LANES)
                cosine = cols_tab[0, pl.ds(layer, 1), cols]
                sine = cols_tab[1, pl.ds(layer, 1), cols]
                turned_real.append(real * cosine - imag * sine)
                turned_imag.append(real * sine + imag * cosine)
            layers_ref[layer, rows, pl.ds(0, LANES)] = jnp.concatenate(turned_real).astype(
                jnp.bfloat16
            )
            layers_ref[layer, rows, pl.ds(LANES, LANES)] = jnp.concatenate(turned_imag).astype(
                jnp.bfloat16
            )
    for block in range(blocks):
        sums = jnp.dot(layers_ref[planes[block]], kernels[block], preferred_element_type=jnp.float32)
        total_real = jnp.zeros((held, LANES), jnp.float32)
        total_imag = jnp.zeros((held, LANES), jnp.float32)
        for part in range(wide):
            sum_real = sums[part * held : (part + 1) * held, :LANES]
            sum_imag = sums[part * held : (part + 1) * held, LANES:]
            cosine = coarse[block, 0, pl.ds(part, 1), :]
            sine = coarse[block, 1, pl.ds(part, 1), :]
            total_real = total_real + (sum_real * cosine - sum_imag * sine)
            total_imag = total_imag + (sum_real * sine + sum_imag * cosine)
        row_cos = rows_tab[block, 0]
        row_sin = rows_tab[block, 1]
        vis_real = jnp.sum(row_cos * total_real - row_sin * total_imag, axis=0, keepdims=True)
        vis_imag = jnp.sum(row_cos * total_imag + row_sin * total_real, axis=0, keepdims=True)
        for part, value in enumerate((vis_real, vis_imag)):
            spot = (0, 0, block, pl.ds(part, 1), slice(None))
            out[spot] = value


def in_smem():
    return pl.BlockSpec(memory_space=pltpu.SMEM)


def in_vmem():
    return pl.BlockSpec(memory_space=pltpu.VMEM)


def kept(value):
    return pltpu.with_memory_space_constraint(value, pltpu.VMEM)


LIMIT = pltpu.CompilerParams(vmem_limit_bytes=16 << 20)


def per_device(
    sky_image, col_off, row_off, layer_counts, w_steps, live_blocks, block_codes, vis_coords
):
    rows_here, facet_cols = sky_image.shape
    num_cols = lax.axis_size("fx")
    num_rows = lax.axis_size("fy")
    half_z = num_cols // 2
    half_y = num_rows // 2
    total_cols = facet_cols * num_cols
    total_rows = rows_here * num_rows
    rows_grid = total_rows
    fine_cols = total_cols // LANES
    facet_rows = facet_cols // fine_cols
    wide = SG // LANES
    blocks = block_codes.shape[2]
    vis_count = vis_coords.shape[-1]
    layers = w_steps.shape[2]
    f32, bf16 = jnp.float32, jnp.bfloat16

    def exchange(value, flip, other_flip):
        pairs = [
            (i, i ^ (flip if i % 2 else other_flip)) for i in range(num_cols * num_rows)
        ]
        return lax.ppermute(value, ("fx", "fy"), pairs)

    near_flip = 2 * num_rows
    passed_sky = exchange(sky_image, 1, 1)
    arguments = (
        sky_image, vis_coords, col_off, row_off, w_steps, block_codes
    )
    own_sky, coords, *scalars = pl.pallas_call(
        load_kernel,
        name="load",
        out_shape=(
            pltpu.VMEM((rows_here, facet_rows, fine_cols), bf16),
            pltpu.VMEM(vis_coords.shape, f32),
            *(pltpu.SMEM(value.shape, value.dtype) for value in arguments[2:]),
        ),
        in_specs=[pl.BlockSpec(memory_space=pl.ANY)] * len(arguments),
        out_specs=(in_vmem(),) * 2 + (in_smem(),) * (len(arguments) - 2),
        scratch_shapes=[
            pltpu.VMEM(sky_image.shape, f32),
            pltpu.VMEM((rows_here * facet_cols // LANES, LANES), f32),
            pltpu.SemaphoreType.DMA((len(arguments),)),
        ],
        compiler_params=LIMIT,
    )(*(pltpu.with_memory_space_constraint(value, pltpu.HBM) for value in arguments))
    coords = kept(coords)
    col_off, row_off, w_steps, block_codes = (
        pltpu.with_memory_space_constraint(value, pltpu.SMEM) for value in scalars
    )
    chip_sky = pl.pallas_call(
        pack_kernel,
        name="pack",
        out_shape=pltpu.VMEM((2, rows_here, facet_rows, fine_cols), bf16),
        in_specs=[in_vmem()] * 2,
        out_specs=in_vmem(),
        scratch_shapes=[pltpu.VMEM((rows_here * facet_cols // LANES, LANES), f32)],
        compiler_params=LIMIT,
    )(kept(own_sky), kept(passed_sky))
    pieces = [chip_sky]
    for slot in range(1, half_z):
        pieces.append(exchange(chip_sky, 2 * slot * num_rows, near_flip))

    first, twiddle, second = pl.pallas_call(
        functools.partial(
            column_tables_kernel,
            (half_z, facet_rows, fine_cols, total_cols, wide, 1.0 / math.sqrt(total_cols)),
        ),
        name="column_tables",
        out_shape=(
            pltpu.VMEM((half_z * facet_rows, 2 * LANES), bf16),
            pltpu.VMEM((2, fine_cols, 2 * LANES), f32),
            pltpu.VMEM((2 * wide, 2 * fine_cols), bf16),
        ),
        in_specs=[in_smem()],
        out_specs=(in_vmem(),) * 3,
        compiler_params=LIMIT,
    )(col_off)

    limits = jnp.where(
        lax.broadcasted_iota(jnp.int32, (1, LANES), 1) == 0, layer_counts, live_blocks
    )
    *tables, planes = pl.pallas_call(
        functools.partial(
            vis_tables_kernel,
            (
                half_y,
                rows_here,
                num_rows,
                rows_grid,
                SG,
                blocks,
                1.0 / math.sqrt(total_rows),
                1.0 / math.sqrt(rows_grid * SG),
            ),
        ),
        name="vis_tables",
        out_shape=(
            pltpu.VMEM((2, layers, SG), f32),
            pltpu.VMEM((blocks, 2 * LANES, 2 * vis_count), bf16),
            pltpu.VMEM((blocks, 2, wide, vis_count), f32),
            pltpu.VMEM((blocks, 2, rows_grid, vis_count), f32),
            pltpu.SMEM((blocks,), jnp.int32),
        ),
        in_specs=[in_smem()] * 3 + [in_vmem()] * 2,
        out_specs=(in_vmem(),) * 4 + (in_smem(),),
        scratch_shapes=[
            pltpu.SMEM((1, LANES), jnp.int32),
            pltpu.VMEM((2 * rows_grid, blocks * vis_count), bf16),
            pltpu.SemaphoreType.DMA,
        ],
        compiler_params=LIMIT,
    )(row_off, w_steps, block_codes, kept(limits), coords)

    band_shape = pltpu.VMEM((2, rows_here, 2 * wide, LANES), bf16)
    own_band, other_band = pl.pallas_call(
        functools.partial(band_kernel, (half_z, facet_rows, fine_cols, rows_here)),
        name="bands",
        out_shape=(band_shape, band_shape),
        in_specs=[in_smem()] + [in_vmem()] * (half_z + 3),
        out_specs=(in_vmem(),) * 2,
        compiler_params=LIMIT,
    )(col_off, *(kept(value) for value in (*pieces, first, twiddle, second)))

    near, far = [own_band], []
    for slot in range(half_y):
        if slot:
            near.append(exchange(own_band, 2 * slot, near_flip))
        far.append(exchange(other_band, num_rows + 2 * slot, near_flip))
    near, far, tables = lax.optimization_barrier((near, far, tables))
    strips = [
        (one.astype(f32) + two.astype(f32)).astype(bf16) for one, two in zip(near, far)
    ]
    own_strips = jnp.stack(strips)
    passed_strips = exchange(own_strips, 1, 1)

    operands = [kept(value) for value in (own_strips, passed_strips, *tables)]
    return pl.pallas_call(
        functools.partial(degrid_kernel, (total_rows, SG, blocks, layers)),
        name="degrid",
        out_shape=jax.ShapeDtypeStruct(vis_coords.shape, f32),
        in_specs=[in_smem()] + [in_vmem()] * len(operands),
        out_specs=in_vmem(),
        scratch_shapes=[
            pltpu.VMEM((total_rows * 2 * wide, LANES), f32),
            pltpu.VMEM((layers, wide * total_rows, 2 * LANES), bf16),
        ],
        compiler_params=LIMIT,
    )(pltpu.with_memory_space_constraint(planes, pltpu.SMEM), *operands)


def solution(mesh):
    placed = (
        P("fy", "fx"),
        P(),
        P(),
        P("fx", "fy"),
        P("fx", "fy", None),
        P("fx", "fy"),
        P("fx", "fy", None),
        P("fx", "fy", None, None, None),
    )
    return jax.shard_map(
        per_device,
        mesh=mesh,
        in_specs=placed,
        out_specs=P("fx", "fy", None, None, None),
        check_vma=False,
    )
```

```python
import functools
import math

import jax
import jax.numpy as jnp
from jax import lax
from jax.experimental import pallas as pl
from jax.experimental.pallas import tpu as pltpu
from jax.sharding import PartitionSpec as P

SG = 1024
NSKY = 65536

LANES = 128
FINE = 16

COS_POLY = (
    0.9999999890590228,
    -19.73920449945383,
    64.93911745989081,
    -85.45013953079767,
    60.167630950263465,
    -25.967599245923743,
    6.52865815775625,
)
SIN_POLY = (
    6.283184916495428,
    -41.34158923268831,
    81.59994332977429,
    -76.61447253115396,
    41.34288235413569,
    -12.471243534350362,
)


def horner(coefficients, value):
    total = jnp.full_like(value, coefficients[-1])
    for coefficient in coefficients[-2::-1]:
        total = total * value + coefficient
    return total


def turn(fraction):
    square = fraction * fraction
    return horner(COS_POLY, square), fraction * horner(SIN_POLY, square)


def turn_of_int(count, modulus):
    half = modulus // 2
    centred = ((count + half) & (modulus - 1)) - half
    return turn(centred.astype(jnp.float32) * (1.0 / modulus))


def wrap(value):
    return value - jnp.round(value)


def iota(shape, axis):
    return lax.broadcasted_iota(jnp.int32, shape, axis)


def settle(flat, split, target):
    rows, pieces, width = target.shape
    parts = width // LANES
    for piece in range(pieces):
        for part in range(parts):
            split[pl.ds(part * rows * pieces + piece, rows, stride=pieces), :] = flat[
                :, pl.ds((piece * parts + part) * LANES, LANES)
            ]
    for row in range(rows):
        for part in range(parts):
            here = pl.ds((part * rows + row) * pieces, pieces)
            target[row, :, pl.ds(part * LANES, LANES)] = split[here, :].astype(jnp.bfloat16)


def pack_kernel(own, passed, out, split):
    out[0] = own[...]
    settle(passed, split, out.at[1])


def load_kernel(*refs):
    count = (len(refs) - 3) // 2
    sources, (sky_out, *targets) = refs[:count], refs[count : 2 * count]
    landed, split, semaphores = refs[2 * count :]
    copies = [
        pltpu.make_async_copy(source, target, semaphores.at[index])
        for index, (source, target) in enumerate(zip(sources, [landed, *targets]))
    ]
    for copy in copies:
        copy.start()
    copies[0].wait()
    settle(landed, split, sky_out)
    for copy in copies[1:]:
        copy.wait()


def column_tables_kernel(dims, col_off, first, twiddle, second):
    half_z, facet_rows, fine_cols, total_cols, wide, scale = dims
    here = lax.axis_index("fx")
    for slot in range(half_z):
        row = facet_rows * (here ^ (2 * slot)) + iota((facet_rows, LANES), 0)
        cosine, sine = turn_of_int(row * iota((facet_rows, LANES), 1), LANES)
        rows = pl.ds(slot * facet_rows, facet_rows)
        first[rows, pl.ds(0, LANES)] = cosine.astype(jnp.bfloat16)
        first[rows, pl.ds(LANES, LANES)] = (-sine).astype(jnp.bfloat16)
    for target in range(2):
        offset = col_off[here ^ target]
        residue = iota((fine_cols, LANES), 1)
        step = (residue - offset) & (LANES - 1)
        cosine, sine = turn_of_int(iota((fine_cols, LANES), 0) * (offset + step), total_cols)
        cols = pl.ds(target * LANES, LANES)
        twiddle[0, :, cols] = cosine * scale
        twiddle[1, :, cols] = sine * (-scale)
    cosine, sine = turn_of_int(iota((wide, fine_cols), 0) * iota((wide, fine_cols), 1), fine_cols)
    second[pl.ds(0, wide), pl.ds(0, fine_cols)] = cosine.astype(jnp.bfloat16)
    second[pl.ds(0, wide), pl.ds(fine_cols, fine_cols)] = sine.astype(jnp.bfloat16)
    second[pl.ds(wide, wide), pl.ds(0, fine_cols)] = (-sine).astype(jnp.bfloat16)
    second[pl.ds(wide, wide), pl.ds(fine_cols, fine_cols)] = cosine.astype(jnp.bfloat16)


def slot_order(half_z):
    return [*range(min(2, half_z)), *range(half_z - 1, 1, -1)]


def band_kernel(dims, col_off, *refs):
    half_z, facet_rows, fine_cols, rows_here = dims
    here = lax.axis_index("fx")
    shifts = [(-col_off[here ^ target]) & (LANES - 1) for target in range(2)]
    pieces = [refs[place] for place in slot_order(half_z)]
    first, twiddle, second, own_out, other_out = refs[half_z:]
    twist_real = twiddle[0]
    twist_imag = twiddle[1]
    for held in range(2):
        stacked = jnp.concatenate(
            [
                jnp.concatenate([piece[held, row] for piece in pieces], axis=0)
                for row in range(rows_here)
            ],
            axis=1,
        )
        spread = lax.dot_general(
            stacked, first[...], (((0,), (0,)), ((), ())), preferred_element_type=jnp.float32
        )
        for row in range(rows_here):
            part = spread[row * fine_cols : (row + 1) * fine_cols]
            part_real = jnp.concatenate([part[:, :LANES]] * 2, axis=1)
            part_imag = jnp.concatenate([part[:, LANES:]] * 2, axis=1)
            turned = jnp.concatenate(
                [
                    part_real * twist_real - part_imag * twist_imag,
                    part_real * twist_imag + part_imag * twist_real,
                ],
                axis=0,
            ).astype(jnp.bfloat16)
            bands = jnp.dot(second[...], turned, preferred_element_type=jnp.float32)
            for target, out in enumerate((own_out, other_out)):
                band = bands[:, target * LANES : (target + 1) * LANES]
                out[held, row] = pltpu.roll(band, shifts[target], 1).astype(jnp.bfloat16)


def vis_tables_kernel(
    dims, row_off, steps, codes, limits_in, coords,
    cols_out, kernels, coarse_out, rows_out, planes, limits, u_tab, semaphore,
):
    half_y, rows_here, num_rows, rows_grid, cols_grid, blocks, row_scale, vis_scale = dims
    here = lax.axis_index("fy")
    fetch = pltpu.make_async_copy(limits_in, limits, semaphore)
    fetch.start()
    shape = (2 * rows_grid, 2 * rows_grid)
    order = iota(shape, 0)
    imag_out = order // rows_grid
    slot = (order // (2 * rows_here)) % half_y
    owner = ((here | 1) ^ (2 * slot)) - (order // rows_here) % 2
    sky_row = owner * (NSKY // num_rows) + order % rows_here
    column = iota(shape, 1)
    imag_in = column // rows_grid
    wave = row_off[here] + column % rows_grid
    cosine, sine = turn_of_int(sky_row * (wave & (NSKY - 1)), NSKY)
    cross = jnp.where(imag_out == 0, sine, -sine)
    row_weights = (jnp.where(imag_in == imag_out, cosine, cross) * row_scale).astype(jnp.bfloat16)
    layers = steps.shape[2]
    depths = []
    depth = steps[0, 0, 0]
    for layer in range(layers):
        if layer:
            depth = depth + steps[0, 0, layer]
        depths.append(depth)
    centre = iota((1, cols_grid), 1) - cols_grid // 2
    squares = centre * centre
    phases = jnp.concatenate([depth * squares for depth in depths], axis=0)
    cosine, sine = turn_of_int(phases, 2 * cols_grid)
    cols_out[0] = cosine
    cols_out[1] = sine
    fetch.wait()
    coarse_count = cols_grid // LANES
    mids = LANES // FINE
    row_index = iota((rows_grid, LANES), 0)
    row_centre = row_index - rows_grid // 2
    row_squares = row_centre * row_centre
    for block in range(blocks):
        plane = lax.rem(codes[0, 0, block], limits[0, 0])
        planes[block] = plane
        depth = depths[0]
        for layer in range(1, layers):
            depth = jnp.where(plane >= layer, depths[layer], depth)
        u_pos = coords[0, 0, block, pl.ds(0, 1), :]
        v_pos = coords[0, 0, block, pl.ds(1, 1), :]
        half = cols_grid
        screen = ((depth * row_squares + half) & (2 * cols_grid - 1)) - half
        angle = wrap(row_index.astype(jnp.float32) * u_pos) + screen.astype(jnp.float32) * (
            1.0 / (2 * cols_grid)
        )
        cosine, sine = turn(wrap(angle))
        weight = jnp.where(block < limits[0, 1], vis_scale, 0.0)
        spot = pl.ds(block * LANES, LANES)
        u_tab[pl.ds(0, rows_grid), spot] = (cosine * weight).astype(jnp.bfloat16)
        u_tab[pl.ds(rows_grid, rows_grid), spot] = (sine * weight).astype(jnp.bfloat16)
        steps_wide = iota((coarse_count, LANES), 0).astype(jnp.float32)
        cosine, sine = turn(wrap(steps_wide * wrap(v_pos * float(LANES))))
        coarse_out[block, 0] = cosine
        coarse_out[block, 1] = sine
        steps_mid = iota((mids, LANES), 0).astype(jnp.float32)
        mid_cos, mid_sin = turn(wrap(steps_mid * wrap(v_pos * float(FINE))))
        steps_fine = iota((FINE, LANES), 0).astype(jnp.float32)
        fine_cos, fine_sin = turn(wrap(steps_fine * v_pos))
        for mid in range(mids):
            head_cos = mid_cos[mid : mid + 1]
            head_sin = mid_sin[mid : mid + 1]
            real = (head_cos * fine_cos - head_sin * fine_sin).astype(jnp.bfloat16)
            imag = (head_sin * fine_cos + head_cos * fine_sin).astype(jnp.bfloat16)
            upper = pl.ds(mid * FINE, FINE)
            lower = pl.ds(LANES + mid * FINE, FINE)
            kernels[block, upper, pl.ds(0, LANES)] = real
            kernels[block, upper, pl.ds(LANES, LANES)] = imag
            kernels[block, lower, pl.ds(0, LANES)] = -imag
            kernels[block, lower, pl.ds(LANES, LANES)] = real
    weights = jnp.dot(row_weights, u_tab[...], preferred_element_type=jnp.float32)
    for block in range(blocks):
        for part in range(2):
            rows_out[block, part] = weights[
                part * rows_grid : (part + 1) * rows_grid, block * LANES : (block + 1) * LANES
            ]


def degrid_kernel(
    dims, planes, local, passed, cols_tab, kernels, coarse, rows_tab, out, strips, layers_ref
):
    held, cols_grid, blocks, layers = dims
    wide = cols_grid // LANES
    lead = lax.axis_index("fy") % 2 == 1
    size = 2 * wide
    for index in range(held):
        spot = (index // (local.shape[1] * local.shape[2]),
                index // local.shape[2] % local.shape[1], index % local.shape[2])
        strips[pl.ds(index * size, size), :] = jnp.where(
            lead, local[spot].astype(jnp.float32), passed[spot].astype(jnp.float32)
        )
    for part in range(0, wide, 2):
        pair = []
        for col in (part, part + 1):
            real = strips[pl.ds(col, held, stride=2 * wide), :]
            imag = strips[pl.ds(wide + col, held, stride=2 * wide), :]
            pair.append((col, real, imag))
        rows = pl.ds(part * held, 2 * held)
        for layer in range(layers):
            turned_real, turned_imag = [], []
            for col, real, imag in pair:
                cols = pl.ds(col * LANES, LANES)
                cosine = cols_tab[0, pl.ds(layer, 1), cols]
                sine = cols_tab[1, pl.ds(layer, 1), cols]
                turned_real.append(real * cosine - imag * sine)
                turned_imag.append(real * sine + imag * cosine)
            layers_ref[layer, rows, pl.ds(0, LANES)] = jnp.concatenate(turned_real).astype(
                jnp.bfloat16
            )
            layers_ref[layer, rows, pl.ds(LANES, LANES)] = jnp.concatenate(turned_imag).astype(
                jnp.bfloat16
            )
    for block in range(blocks):
        sums = jnp.dot(layers_ref[planes[block]], kernels[block], preferred_element_type=jnp.float32)
        total_real = jnp.zeros((held, LANES), jnp.float32)
        total_imag = jnp.zeros((held, LANES), jnp.float32)
        for part in range(wide):
            sum_real = sums[part * held : (part + 1) * held, :LANES]
            sum_imag = sums[part * held : (part + 1) * held, LANES:]
            cosine = coarse[block, 0, pl.ds(part, 1), :]
            sine = coarse[block, 1, pl.ds(part, 1), :]
            total_real = total_real + (sum_real * cosine - sum_imag * sine)
            total_imag = total_imag + (sum_real * sine + sum_imag * cosine)
        row_cos = rows_tab[block, 0]
        row_sin = rows_tab[block, 1]
        vis_real = jnp.sum(row_cos * total_real - row_sin * total_imag, axis=0, keepdims=True)
        vis_imag = jnp.sum(row_cos * total_imag + row_sin * total_real, axis=0, keepdims=True)
        for part, value in enumerate((vis_real, vis_imag)):
            spot = (0, 0, block, pl.ds(part, 1), slice(None))
            out[spot] = value


def in_smem():
    return pl.BlockSpec(memory_space=pltpu.SMEM)


def in_vmem():
    return pl.BlockSpec(memory_space=pltpu.VMEM)


def kept(value):
    return pltpu.with_memory_space_constraint(value, pltpu.VMEM)


LIMIT = pltpu.CompilerParams(vmem_limit_bytes=16 << 20)


def per_device(
    sky_image, col_off, row_off, layer_counts, w_steps, live_blocks, block_codes, vis_coords
):
    rows_here, facet_cols = sky_image.shape
    num_cols = lax.axis_size("fx")
    num_rows = lax.axis_size("fy")
    half_z = num_cols // 2
    half_y = num_rows // 2
    total_cols = facet_cols * num_cols
    total_rows = rows_here * num_rows
    rows_grid = total_rows
    fine_cols = total_cols // LANES
    facet_rows = facet_cols // fine_cols
    wide = SG // LANES
    blocks = block_codes.shape[2]
    vis_count = vis_coords.shape[-1]
    layers = w_steps.shape[2]
    f32, bf16 = jnp.float32, jnp.bfloat16

    def exchange(value, flip, other_flip):
        pairs = [
            (i, i ^ (flip if i % 2 else other_flip)) for i in range(num_cols * num_rows)
        ]
        return lax.ppermute(value, ("fx", "fy"), pairs)

    near_flip = 2 * num_rows
    passed_sky = exchange(sky_image, 1, 1)
    arguments = (
        sky_image, vis_coords, col_off, row_off, w_steps, block_codes
    )
    own_sky, coords, *scalars = pl.pallas_call(
        load_kernel,
        name="load",
        out_shape=(
            pltpu.VMEM((rows_here, facet_rows, fine_cols), bf16),
            pltpu.VMEM(vis_coords.shape, f32),
            *(pltpu.SMEM(value.shape, value.dtype) for value in arguments[2:]),
        ),
        in_specs=[pl.BlockSpec(memory_space=pl.ANY)] * len(arguments),
        out_specs=(in_vmem(),) * 2 + (in_smem(),) * (len(arguments) - 2),
        scratch_shapes=[
            pltpu.VMEM(sky_image.shape, f32),
            pltpu.VMEM((rows_here * facet_cols // LANES, LANES), f32),
            pltpu.SemaphoreType.DMA((len(arguments),)),
        ],
        compiler_params=LIMIT,
    )(*(pltpu.with_memory_space_constraint(value, pltpu.HBM) for value in arguments))
    coords = kept(coords)
    col_off, row_off, w_steps, block_codes = (
        pltpu.with_memory_space_constraint(value, pltpu.SMEM) for value in scalars
    )
    chip_sky = pl.pallas_call(
        pack_kernel,
        name="pack",
        out_shape=pltpu.VMEM((2, rows_here, facet_rows, fine_cols), bf16),
        in_specs=[in_vmem()] * 2,
        out_specs=in_vmem(),
        scratch_shapes=[pltpu.VMEM((rows_here * facet_cols // LANES, LANES), f32)],
        compiler_params=LIMIT,
    )(kept(own_sky), kept(passed_sky))
    pieces = [chip_sky]
    for slot in range(1, half_z):
        pieces.append(exchange(chip_sky, 2 * slot * num_rows, near_flip))

    operands = [pieces[slot] for slot in slot_order(half_z)]

    first, twiddle, second = pl.pallas_call(
        functools.partial(
            column_tables_kernel,
            (half_z, facet_rows, fine_cols, total_cols, wide, 1.0 / math.sqrt(total_cols)),
        ),
        name="column_tables",
        out_shape=(
            pltpu.VMEM((half_z * facet_rows, 2 * LANES), bf16),
            pltpu.VMEM((2, fine_cols, 2 * LANES), f32),
            pltpu.VMEM((2 * wide, 2 * fine_cols), bf16),
        ),
        in_specs=[in_smem()],
        out_specs=(in_vmem(),) * 3,
        compiler_params=LIMIT,
    )(col_off)

    limits = jnp.where(
        lax.broadcasted_iota(jnp.int32, (1, LANES), 1) == 0, layer_counts, live_blocks
    )
    *tables, planes = pl.pallas_call(
        functools.partial(
            vis_tables_kernel,
            (
                half_y,
                rows_here,
                num_rows,
                rows_grid,
                SG,
                blocks,
                1.0 / math.sqrt(total_rows),
                1.0 / math.sqrt(rows_grid * SG),
            ),
        ),
        name="vis_tables",
        out_shape=(
            pltpu.VMEM((2, layers, SG), f32),
            pltpu.VMEM((blocks, 2 * LANES, 2 * vis_count), bf16),
            pltpu.VMEM((blocks, 2, wide, vis_count), f32),
            pltpu.VMEM((blocks, 2, rows_grid, vis_count), f32),
            pltpu.SMEM((blocks,), jnp.int32),
        ),
        in_specs=[in_smem()] * 3 + [in_vmem()] * 2,
        out_specs=(in_vmem(),) * 4 + (in_smem(),),
        scratch_shapes=[
            pltpu.SMEM((1, LANES), jnp.int32),
            pltpu.VMEM((2 * rows_grid, blocks * vis_count), bf16),
            pltpu.SemaphoreType.DMA,
        ],
        compiler_params=LIMIT,
    )(row_off, w_steps, block_codes, kept(limits), coords)

    band_shape = pltpu.VMEM((2, rows_here, 2 * wide, LANES), bf16)
    own_band, other_band = pl.pallas_call(
        functools.partial(band_kernel, (half_z, facet_rows, fine_cols, rows_here)),
        name="bands",
        out_shape=(band_shape, band_shape),
        in_specs=[in_smem()] + [in_vmem()] * (half_z + 3),
        out_specs=(in_vmem(),) * 2,
        compiler_params=LIMIT,
    )(col_off, *(kept(value) for value in (*operands, first, twiddle, second)))

    near, far = [own_band], []
    for slot in range(half_y):
        if slot:
            near.append(exchange(own_band, 2 * slot, near_flip))
        far.append(exchange(other_band, num_rows + 2 * slot, near_flip))
    near, far, tables = lax.optimization_barrier((near, far, tables))
    strips = [
        (one.astype(f32) + two.astype(f32)).astype(bf16) for one, two in zip(near, far)
    ]
    own_strips = jnp.stack(strips)
    passed_strips = exchange(own_strips, 1, 1)

    operands = [kept(value) for value in (own_strips, passed_strips, *tables)]
    return pl.pallas_call(
        functools.partial(degrid_kernel, (total_rows, SG, blocks, layers)),
        name="degrid",
        out_shape=jax.ShapeDtypeStruct(vis_coords.shape, f32),
        in_specs=[in_smem()] + [in_vmem()] * len(operands),
        out_specs=in_vmem(),
        scratch_shapes=[
            pltpu.VMEM((total_rows * 2 * wide, LANES), f32),
            pltpu.VMEM((layers, wide * total_rows, 2 * LANES), bf16),
        ],
        compiler_params=LIMIT,
    )(pltpu.with_memory_space_constraint(planes, pltpu.SMEM), *operands)


def solution(mesh):
    placed = (
        P("fy", "fx"),
        P(),
        P(),
        P("fx", "fy"),
        P("fx", "fy", None),
        P("fx", "fy"),
        P("fx", "fy", None),
        P("fx", "fy", None, None, None),
    )
    return jax.shard_map(
        per_device,
        mesh=mesh,
        in_specs=placed,
        out_specs=P("fx", "fy", None, None, None),
        check_vma=False,
    )
```

```python
import functools
import math

import jax
import jax.numpy as jnp
from jax import lax
from jax.experimental import pallas as pl
from jax.experimental.pallas import tpu as pltpu
from jax.sharding import PartitionSpec as P

SG = 1024
NSKY = 65536

LANES = 128
FINE = 16

COS_POLY = (
    0.9999999890590228,
    -19.73920449945383,
    64.93911745989081,
    -85.45013953079767,
    60.167630950263465,
    -25.967599245923743,
    6.52865815775625,
)
SIN_POLY = (
    6.283184916495428,
    -41.34158923268831,
    81.59994332977429,
    -76.61447253115396,
    41.34288235413569,
    -12.471243534350362,
)


def horner(coefficients, value):
    total = jnp.full_like(value, coefficients[-1])
    for coefficient in coefficients[-2::-1]:
        total = total * value + coefficient
    return total


def turn(fraction):
    square = fraction * fraction
    return horner(COS_POLY, square), fraction * horner(SIN_POLY, square)


def turn_of_int(count, modulus):
    half = modulus // 2
    centred = ((count + half) & (modulus - 1)) - half
    return turn(centred.astype(jnp.float32) * (1.0 / modulus))


def wrap(value):
    return value - jnp.round(value)


def iota(shape, axis):
    return lax.broadcasted_iota(jnp.int32, shape, axis)


def settle(flat, split, target):
    rows, pieces, width = target.shape
    parts = width // LANES
    for piece in range(pieces):
        for part in range(parts):
            split[pl.ds(part * rows * pieces + piece, rows, stride=pieces), :] = flat[
                :, pl.ds((piece * parts + part) * LANES, LANES)
            ]
    for row in range(rows):
        for part in range(parts):
            here = pl.ds((part * rows + row) * pieces, pieces)
            target[row, :, pl.ds(part * LANES, LANES)] = split[here, :].astype(jnp.bfloat16)


def pack_kernel(own, passed, out, split):
    out[0] = own[...]
    settle(passed, split, out.at[1])


def load_kernel(*refs):
    count = (len(refs) - 3) // 2
    sources, (sky_out, *targets) = refs[:count], refs[count : 2 * count]
    landed, split, semaphores = refs[2 * count :]
    copies = [
        pltpu.make_async_copy(source, target, semaphores.at[index])
        for index, (source, target) in enumerate(zip(sources, [landed, *targets]))
    ]
    for copy in copies:
        copy.start()
    copies[0].wait()
    settle(landed, split, sky_out)
    for copy in copies[1:]:
        copy.wait()


def column_tables_kernel(dims, col_off, first, twiddle, second):
    half_z, facet_rows, fine_cols, total_cols, wide, scale = dims
    here = lax.axis_index("fx")
    for slot in range(half_z):
        row = facet_rows * (here ^ (2 * slot)) + iota((facet_rows, LANES), 0)
        cosine, sine = turn_of_int(row * iota((facet_rows, LANES), 1), LANES)
        rows = pl.ds(slot * facet_rows, facet_rows)
        first[rows, pl.ds(0, LANES)] = cosine.astype(jnp.bfloat16)
        first[rows, pl.ds(LANES, LANES)] = (-sine).astype(jnp.bfloat16)
    for target in range(2):
        offset = col_off[here ^ target]
        residue = iota((fine_cols, LANES), 1)
        step = (residue - offset) & (LANES - 1)
        cosine, sine = turn_of_int(iota((fine_cols, LANES), 0) * (offset + step), total_cols)
        cols = pl.ds(target * LANES, LANES)
        twiddle[0, :, cols] = cosine * scale
        twiddle[1, :, cols] = sine * (-scale)
    cosine, sine = turn_of_int(iota((wide, fine_cols), 0) * iota((wide, fine_cols), 1), fine_cols)
    second[pl.ds(0, wide), pl.ds(0, fine_cols)] = cosine.astype(jnp.bfloat16)
    second[pl.ds(0, wide), pl.ds(fine_cols, fine_cols)] = sine.astype(jnp.bfloat16)
    second[pl.ds(wide, wide), pl.ds(0, fine_cols)] = (-sine).astype(jnp.bfloat16)
    second[pl.ds(wide, wide), pl.ds(fine_cols, fine_cols)] = cosine.astype(jnp.bfloat16)


def slot_order(half_z):
    return [*range(min(2, half_z)), *range(half_z - 1, 1, -1)]


def band_kernel(dims, col_off, *refs):
    half_z, facet_rows, fine_cols, rows_here = dims
    here = lax.axis_index("fx")
    shifts = [(-col_off[here ^ target]) & (LANES - 1) for target in range(2)]
    pieces = [refs[place] for place in slot_order(half_z)]
    first, twiddle, second, own_out, other_out = refs[half_z:]
    twist_real = twiddle[0]
    twist_imag = twiddle[1]
    for held in range(2):
        stacked = jnp.concatenate(
            [
                jnp.concatenate([piece[held, row] for piece in pieces], axis=0)
                for row in range(rows_here)
            ],
            axis=1,
        )
        spread = lax.dot_general(
            stacked, first[...], (((0,), (0,)), ((), ())), preferred_element_type=jnp.float32
        )
        for row in range(rows_here):
            part = spread[row * fine_cols : (row + 1) * fine_cols]
            part_real = jnp.concatenate([part[:, :LANES]] * 2, axis=1)
            part_imag = jnp.concatenate([part[:, LANES:]] * 2, axis=1)
            turned = jnp.concatenate(
                [
                    part_real * twist_real - part_imag * twist_imag,
                    part_real * twist_imag + part_imag * twist_real,
                ],
                axis=0,
            ).astype(jnp.bfloat16)
            bands = jnp.dot(second[...], turned, preferred_element_type=jnp.float32)
            for target, out in enumerate((own_out, other_out)):
                band = bands[:, target * LANES : (target + 1) * LANES]
                out[held, row] = pltpu.roll(band, shifts[target], 1).astype(jnp.bfloat16)


def vis_tables_kernel(
    dims, row_off, steps, codes, limits_in, coords,
    cols_out, kernels, coarse_out, rows_out, planes, limits, u_tab, semaphore,
):
    half_y, rows_here, num_rows, rows_grid, cols_grid, blocks, row_scale, vis_scale = dims
    here = lax.axis_index("fy")
    fetch = pltpu.make_async_copy(limits_in, limits, semaphore)
    fetch.start()
    shape = (2 * rows_grid, 2 * rows_grid)
    order = iota(shape, 0)
    imag_out = order // rows_grid
    slot = (order // (2 * rows_here)) % half_y
    owner = ((here | 1) ^ (2 * slot)) - (order // rows_here) % 2
    sky_row = owner * (NSKY // num_rows) + order % rows_here
    column = iota(shape, 1)
    imag_in = column // rows_grid
    wave = row_off[here] + column % rows_grid
    cosine, sine = turn_of_int(sky_row * (wave & (NSKY - 1)), NSKY)
    cross = jnp.where(imag_out == 0, sine, -sine)
    row_weights = (jnp.where(imag_in == imag_out, cosine, cross) * row_scale).astype(jnp.bfloat16)
    layers = steps.shape[2]
    depths = []
    depth = steps[0, 0, 0]
    for layer in range(layers):
        if layer:
            depth = depth + steps[0, 0, layer]
        depths.append(depth)
    centre = iota((1, cols_grid), 1) - cols_grid // 2
    squares = centre * centre
    phases = jnp.concatenate([depth * squares for depth in depths], axis=0)
    cosine, sine = turn_of_int(phases, 2 * cols_grid)
    cols_out[0] = cosine
    cols_out[1] = sine
    fetch.wait()
    coarse_count = cols_grid // LANES
    mids = LANES // FINE
    row_index = iota((rows_grid, LANES), 0)
    row_centre = row_index - rows_grid // 2
    row_squares = row_centre * row_centre
    for block in range(blocks):
        plane = lax.rem(codes[0, 0, block], limits[0, 0])
        planes[block] = plane
        depth = depths[0]
        for layer in range(1, layers):
            depth = jnp.where(plane >= layer, depths[layer], depth)
        u_pos = coords[0, 0, block, pl.ds(0, 1), :]
        v_pos = coords[0, 0, block, pl.ds(1, 1), :]
        half = cols_grid
        screen = ((depth * row_squares + half) & (2 * cols_grid - 1)) - half
        angle = wrap(row_index.astype(jnp.float32) * u_pos) + screen.astype(jnp.float32) * (
            1.0 / (2 * cols_grid)
        )
        cosine, sine = turn(wrap(angle))
        weight = jnp.where(block < limits[0, 1], vis_scale, 0.0)
        spot = pl.ds(block * LANES, LANES)
        u_tab[pl.ds(0, rows_grid), spot] = (cosine * weight).astype(jnp.bfloat16)
        u_tab[pl.ds(rows_grid, rows_grid), spot] = (sine * weight).astype(jnp.bfloat16)
        steps_wide = iota((coarse_count, LANES), 0).astype(jnp.float32)
        cosine, sine = turn(wrap(steps_wide * wrap(v_pos * float(LANES))))
        coarse_out[block, 0] = cosine
        coarse_out[block, 1] = sine
        steps_mid = iota((mids, LANES), 0).astype(jnp.float32)
        mid_cos, mid_sin = turn(wrap(steps_mid * wrap(v_pos * float(FINE))))
        steps_fine = iota((FINE, LANES), 0).astype(jnp.float32)
        fine_cos, fine_sin = turn(wrap(steps_fine * v_pos))
        for mid in range(mids):
            head_cos = mid_cos[mid : mid + 1]
            head_sin = mid_sin[mid : mid + 1]
            real = (head_cos * fine_cos - head_sin * fine_sin).astype(jnp.bfloat16)
            imag = (head_sin * fine_cos + head_cos * fine_sin).astype(jnp.bfloat16)
            upper = pl.ds(mid * FINE, FINE)
            lower = pl.ds(LANES + mid * FINE, FINE)
            kernels[block, upper, pl.ds(0, LANES)] = real
            kernels[block, upper, pl.ds(LANES, LANES)] = imag
            kernels[block, lower, pl.ds(0, LANES)] = -imag
            kernels[block, lower, pl.ds(LANES, LANES)] = real
    weights = jnp.dot(row_weights, u_tab[...], preferred_element_type=jnp.float32)
    for block in range(blocks):
        for part in range(2):
            rows_out[block, part] = weights[
                part * rows_grid : (part + 1) * rows_grid, block * LANES : (block + 1) * LANES
            ]


def degrid_kernel(
    dims, planes, local, passed, cols_tab, kernels, coarse, rows_tab, out, strips, layers_ref
):
    held, cols_grid, blocks, layers = dims
    wide = cols_grid // LANES
    lead = lax.axis_index("fy") % 2 == 1
    size = 2 * wide
    for index in range(held):
        spot = (index // (local.shape[1] * local.shape[2]),
                index // local.shape[2] % local.shape[1], index % local.shape[2])
        strips[pl.ds(index * size, size), :] = jnp.where(
            lead, local[spot].astype(jnp.float32), passed[spot].astype(jnp.float32)
        )
    for part in range(0, wide, 2):
        pair = []
        for col in (part, part + 1):
            real = strips[pl.ds(col, held, stride=2 * wide), :]
            imag = strips[pl.ds(wide + col, held, stride=2 * wide), :]
            pair.append((col, real, imag))
        rows = pl.ds(part * held, 2 * held)
        for layer in range(layers):
            turned_real, turned_imag = [], []
            for col, real, imag in pair:
                cols = pl.ds(col * LANES, LANES)
                cosine = cols_tab[0, pl.ds(layer, 1), cols]
                sine = cols_tab[1, pl.ds(layer, 1), cols]
                turned_real.append(real * cosine - imag * sine)
                turned_imag.append(real * sine + imag * cosine)
            layers_ref[layer, rows, pl.ds(0, LANES)] = jnp.concatenate(turned_real).astype(
                jnp.bfloat16
            )
            layers_ref[layer, rows, pl.ds(LANES, LANES)] = jnp.concatenate(turned_imag).astype(
                jnp.bfloat16
            )
    for block in range(blocks):
        sums = jnp.dot(layers_ref[planes[block]], kernels[block], preferred_element_type=jnp.float32)
        total_real = jnp.zeros((held, LANES), jnp.float32)
        total_imag = jnp.zeros((held, LANES), jnp.float32)
        for part in range(wide):
            sum_real = sums[part * held : (part + 1) * held, :LANES]
            sum_imag = sums[part * held : (part + 1) * held, LANES:]
            cosine = coarse[block, 0, pl.ds(part, 1), :]
            sine = coarse[block, 1, pl.ds(part, 1), :]
            total_real = total_real + (sum_real * cosine - sum_imag * sine)
            total_imag = total_imag + (sum_real * sine + sum_imag * cosine)
        row_cos = rows_tab[block, 0]
        row_sin = rows_tab[block, 1]
        vis_real = jnp.sum(row_cos * total_real - row_sin * total_imag, axis=0, keepdims=True)
        vis_imag = jnp.sum(row_cos * total_imag + row_sin * total_real, axis=0, keepdims=True)
        for part, value in enumerate((vis_real, vis_imag)):
            spot = (0, 0, block, pl.ds(part, 1), slice(None))
            out[spot] = value


def in_smem():
    return pl.BlockSpec(memory_space=pltpu.SMEM)


def in_vmem():
    return pl.BlockSpec(memory_space=pltpu.VMEM)


def kept(value):
    return pltpu.with_memory_space_constraint(value, pltpu.VMEM)


LIMIT = pltpu.CompilerParams(vmem_limit_bytes=16 << 20)


def per_device(
    sky_image, col_off, row_off, layer_counts, w_steps, live_blocks, block_codes, vis_coords
):
    rows_here, facet_cols = sky_image.shape
    num_cols = lax.axis_size("fx")
    num_rows = lax.axis_size("fy")
    half_z = num_cols // 2
    half_y = num_rows // 2
    total_cols = facet_cols * num_cols
    total_rows = rows_here * num_rows
    rows_grid = total_rows
    fine_cols = total_cols // LANES
    facet_rows = facet_cols // fine_cols
    wide = SG // LANES
    blocks = block_codes.shape[2]
    vis_count = vis_coords.shape[-1]
    layers = w_steps.shape[2]
    f32, bf16 = jnp.float32, jnp.bfloat16

    def exchange(value, flip, other_flip):
        pairs = [
            (i, i ^ (flip if i % 2 else other_flip)) for i in range(num_cols * num_rows)
        ]
        return lax.ppermute(value, ("fx", "fy"), pairs)

    near_flip = 2 * num_rows
    passed_sky = exchange(sky_image, 1, 1)
    arguments = (
        sky_image, vis_coords, col_off, row_off, w_steps, block_codes
    )
    own_sky, coords, *scalars = pl.pallas_call(
        load_kernel,
        name="load",
        out_shape=(
            pltpu.VMEM((rows_here, facet_rows, fine_cols), bf16),
            pltpu.VMEM(vis_coords.shape, f32),
            *(pltpu.SMEM(value.shape, value.dtype) for value in arguments[2:]),
        ),
        in_specs=[pl.BlockSpec(memory_space=pl.ANY)] * len(arguments),
        out_specs=(in_vmem(),) * 2 + (in_smem(),) * (len(arguments) - 2),
        scratch_shapes=[
            pltpu.VMEM(sky_image.shape, f32),
            pltpu.VMEM((rows_here * facet_cols // LANES, LANES), f32),
            pltpu.SemaphoreType.DMA((len(arguments),)),
        ],
        compiler_params=LIMIT,
    )(*(pltpu.with_memory_space_constraint(value, pltpu.HBM) for value in arguments))
    coords = kept(coords)
    col_off, row_off, w_steps, block_codes = (
        pltpu.with_memory_space_constraint(value, pltpu.SMEM) for value in scalars
    )
    chip_sky = pl.pallas_call(
        pack_kernel,
        name="pack",
        out_shape=pltpu.VMEM((2, rows_here, facet_rows, fine_cols), bf16),
        in_specs=[in_vmem()] * 2,
        out_specs=in_vmem(),
        scratch_shapes=[pltpu.VMEM((rows_here * facet_cols // LANES, LANES), f32)],
        compiler_params=LIMIT,
    )(kept(own_sky), kept(passed_sky))
    pieces = [chip_sky]
    for slot in range(1, half_z):
        pieces.append(exchange(chip_sky, 2 * slot * num_rows, 2))

    operands = [pieces[slot] for slot in slot_order(half_z)]

    first, twiddle, second = pl.pallas_call(
        functools.partial(
            column_tables_kernel,
            (half_z, facet_rows, fine_cols, total_cols, wide, 1.0 / math.sqrt(total_cols)),
        ),
        name="column_tables",
        out_shape=(
            pltpu.VMEM((half_z * facet_rows, 2 * LANES), bf16),
            pltpu.VMEM((2, fine_cols, 2 * LANES), f32),
            pltpu.VMEM((2 * wide, 2 * fine_cols), bf16),
        ),
        in_specs=[in_smem()],
        out_specs=(in_vmem(),) * 3,
        compiler_params=LIMIT,
    )(col_off)

    limits = jnp.where(
        lax.broadcasted_iota(jnp.int32, (1, LANES), 1) == 0, layer_counts, live_blocks
    )
    *tables, planes = pl.pallas_call(
        functools.partial(
            vis_tables_kernel,
            (
                half_y,
                rows_here,
                num_rows,
                rows_grid,
                SG,
                blocks,
                1.0 / math.sqrt(total_rows),
                1.0 / math.sqrt(rows_grid * SG),
            ),
        ),
        name="vis_tables",
        out_shape=(
            pltpu.VMEM((2, layers, SG), f32),
            pltpu.VMEM((blocks, 2 * LANES, 2 * vis_count), bf16),
            pltpu.VMEM((blocks, 2, wide, vis_count), f32),
            pltpu.VMEM((blocks, 2, rows_grid, vis_count), f32),
            pltpu.SMEM((blocks,), jnp.int32),
        ),
        in_specs=[in_smem()] * 3 + [in_vmem()] * 2,
        out_specs=(in_vmem(),) * 4 + (in_smem(),),
        scratch_shapes=[
            pltpu.SMEM((1, LANES), jnp.int32),
            pltpu.VMEM((2 * rows_grid, blocks * vis_count), bf16),
            pltpu.SemaphoreType.DMA,
        ],
        compiler_params=LIMIT,
    )(row_off, w_steps, block_codes, kept(limits), coords)

    band_shape = pltpu.VMEM((2, rows_here, 2 * wide, LANES), bf16)
    own_band, other_band = pl.pallas_call(
        functools.partial(band_kernel, (half_z, facet_rows, fine_cols, rows_here)),
        name="bands",
        out_shape=(band_shape, band_shape),
        in_specs=[in_smem()] + [in_vmem()] * (half_z + 3),
        out_specs=(in_vmem(),) * 2,
        compiler_params=LIMIT,
    )(col_off, *(kept(value) for value in (*operands, first, twiddle, second)))

    near, far = [own_band], []
    for slot in range(half_y):
        if slot:
            near.append(exchange(own_band, 2 * slot, near_flip))
        far.append(exchange(other_band, num_rows + 2 * slot, near_flip))
    near, far, tables = lax.optimization_barrier((near, far, tables))
    strips = [
        (one.astype(f32) + two.astype(f32)).astype(bf16) for one, two in zip(near, far)
    ]
    own_strips = jnp.stack(strips)
    passed_strips = exchange(own_strips, 1, 1)

    operands = [kept(value) for value in (own_strips, passed_strips, *tables)]
    return pl.pallas_call(
        functools.partial(degrid_kernel, (total_rows, SG, blocks, layers)),
        name="degrid",
        out_shape=jax.ShapeDtypeStruct(vis_coords.shape, f32),
        in_specs=[in_smem()] + [in_vmem()] * len(operands),
        out_specs=in_vmem(),
        scratch_shapes=[
            pltpu.VMEM((total_rows * 2 * wide, LANES), f32),
            pltpu.VMEM((layers, wide * total_rows, 2 * LANES), bf16),
        ],
        compiler_params=LIMIT,
    )(pltpu.with_memory_space_constraint(planes, pltpu.SMEM), *operands)


def solution(mesh):
    placed = (
        P("fy", "fx"),
        P(),
        P(),
        P("fx", "fy"),
        P("fx", "fy", None),
        P("fx", "fy"),
        P("fx", "fy", None),
        P("fx", "fy", None, None, None),
    )
    return jax.shard_map(
        per_device,
        mesh=mesh,
        in_specs=placed,
        out_specs=P("fx", "fy", None, None, None),
        check_vma=False,
    )
```

```python
import functools
import math

import jax
import jax.numpy as jnp
from jax import lax
from jax.experimental import pallas as pl
from jax.experimental.pallas import tpu as pltpu
from jax.sharding import PartitionSpec as P

SG = 1024
NSKY = 65536

LANES = 128
FINE = 16

COS_POLY = (
    0.9999999890590228,
    -19.73920449945383,
    64.93911745989081,
    -85.45013953079767,
    60.167630950263465,
    -25.967599245923743,
    6.52865815775625,
)
SIN_POLY = (
    6.283184916495428,
    -41.34158923268831,
    81.59994332977429,
    -76.61447253115396,
    41.34288235413569,
    -12.471243534350362,
)


def horner(coefficients, value):
    total = jnp.full_like(value, coefficients[-1])
    for coefficient in coefficients[-2::-1]:
        total = total * value + coefficient
    return total


def turn(fraction):
    square = fraction * fraction
    return horner(COS_POLY, square), fraction * horner(SIN_POLY, square)


def turn_of_int(count, modulus):
    half = modulus // 2
    centred = ((count + half) & (modulus - 1)) - half
    return turn(centred.astype(jnp.float32) * (1.0 / modulus))


def wrap(value):
    return value - jnp.round(value)


def iota(shape, axis):
    return lax.broadcasted_iota(jnp.int32, shape, axis)


def settle(flat, split, target):
    rows, pieces, width = target.shape
    parts = width // LANES
    for piece in range(pieces):
        for part in range(parts):
            split[pl.ds(part * rows * pieces + piece, rows, stride=pieces), :] = flat[
                :, pl.ds((piece * parts + part) * LANES, LANES)
            ]
    for row in range(rows):
        for part in range(parts):
            here = pl.ds((part * rows + row) * pieces, pieces)
            target[row, :, pl.ds(part * LANES, LANES)] = split[here, :].astype(jnp.bfloat16)


def pack_kernel(own, passed, out, split):
    out[0] = own[...]
    settle(passed, split, out.at[1])


def load_kernel(*refs):
    count = (len(refs) - 3) // 2
    sources, (sky_out, *targets) = refs[:count], refs[count : 2 * count]
    landed, split, semaphores = refs[2 * count :]
    copies = [
        pltpu.make_async_copy(source, target, semaphores.at[index])
        for index, (source, target) in enumerate(zip(sources, [landed, *targets]))
    ]
    for copy in copies:
        copy.start()
    copies[0].wait()
    settle(landed, split, sky_out)
    for copy in copies[1:]:
        copy.wait()


def column_tables_kernel(dims, col_off, first, twiddle, second):
    half_z, facet_rows, fine_cols, total_cols, wide, scale = dims
    here = lax.axis_index("fx")
    for slot in range(half_z):
        row = facet_rows * (here ^ (2 * slot)) + iota((facet_rows, LANES), 0)
        cosine, sine = turn_of_int(row * iota((facet_rows, LANES), 1), LANES)
        rows = pl.ds(slot * facet_rows, facet_rows)
        first[rows, pl.ds(0, LANES)] = cosine.astype(jnp.bfloat16)
        first[rows, pl.ds(LANES, LANES)] = (-sine).astype(jnp.bfloat16)
    for target in range(2):
        offset = col_off[here ^ target]
        residue = iota((fine_cols, LANES), 1)
        step = (residue - offset) & (LANES - 1)
        cosine, sine = turn_of_int(iota((fine_cols, LANES), 0) * (offset + step), total_cols)
        cols = pl.ds(target * LANES, LANES)
        twiddle[0, :, cols] = cosine * scale
        twiddle[1, :, cols] = sine * (-scale)
    cosine, sine = turn_of_int(iota((wide, fine_cols), 0) * iota((wide, fine_cols), 1), fine_cols)
    second[pl.ds(0, wide), pl.ds(0, fine_cols)] = cosine.astype(jnp.bfloat16)
    second[pl.ds(0, wide), pl.ds(fine_cols, fine_cols)] = sine.astype(jnp.bfloat16)
    second[pl.ds(wide, wide), pl.ds(0, fine_cols)] = (-sine).astype(jnp.bfloat16)
    second[pl.ds(wide, wide), pl.ds(fine_cols, fine_cols)] = cosine.astype(jnp.bfloat16)


def slot_order(half_z):
    return [*range(min(2, half_z)), *range(half_z - 1, 1, -1)]


def band_kernel(dims, col_off, *refs):
    half_z, facet_rows, fine_cols, rows_here = dims
    here = lax.axis_index("fx")
    shifts = [(-col_off[here ^ target]) & (LANES - 1) for target in range(2)]
    pieces = [refs[place] for place in slot_order(half_z)]
    first, twiddle, second, own_out, other_out = refs[half_z:]
    twist_real = twiddle[0]
    twist_imag = twiddle[1]
    for held in range(2):
        stacked = jnp.concatenate(
            [
                jnp.concatenate([piece[held, row] for piece in pieces], axis=0)
                for row in range(rows_here)
            ],
            axis=1,
        )
        spread = lax.dot_general(
            stacked, first[...], (((0,), (0,)), ((), ())), preferred_element_type=jnp.float32
        )
        for row in range(rows_here):
            part = spread[row * fine_cols : (row + 1) * fine_cols]
            part_real = jnp.concatenate([part[:, :LANES]] * 2, axis=1)
            part_imag = jnp.concatenate([part[:, LANES:]] * 2, axis=1)
            turned = jnp.concatenate(
                [
                    part_real * twist_real - part_imag * twist_imag,
                    part_real * twist_imag + part_imag * twist_real,
                ],
                axis=0,
            ).astype(jnp.bfloat16)
            bands = jnp.dot(second[...], turned, preferred_element_type=jnp.float32)
            for target, out in enumerate((own_out, other_out)):
                band = bands[:, target * LANES : (target + 1) * LANES]
                out[held, row] = pltpu.roll(band, shifts[target], 1).astype(jnp.bfloat16)


def vis_tables_kernel(
    dims, row_off, steps, codes, limits_in, coords,
    cols_out, kernels, coarse_out, rows_out, planes, limits, u_tab, semaphore,
):
    half_y, rows_here, num_rows, rows_grid, cols_grid, blocks, row_scale, vis_scale = dims
    here = lax.axis_index("fy")
    fetch = pltpu.make_async_copy(limits_in, limits, semaphore)
    fetch.start()
    shape = (2 * rows_grid, 2 * rows_grid)
    order = iota(shape, 0)
    imag_out = order // rows_grid
    slot = (order // (2 * rows_here)) % half_y
    owner = ((here | 1) ^ (2 * slot)) - (order // rows_here) % 2
    sky_row = owner * (NSKY // num_rows) + order % rows_here
    column = iota(shape, 1)
    imag_in = column // rows_grid
    wave = row_off[here] + column % rows_grid
    cosine, sine = turn_of_int(sky_row * (wave & (NSKY - 1)), NSKY)
    cross = jnp.where(imag_out == 0, sine, -sine)
    row_weights = (jnp.where(imag_in == imag_out, cosine, cross) * row_scale).astype(jnp.bfloat16)
    layers = steps.shape[2]
    depths = []
    depth = steps[0, 0, 0]
    for layer in range(layers):
        if layer:
            depth = depth + steps[0, 0, layer]
        depths.append(depth)
    centre = iota((1, cols_grid), 1) - cols_grid // 2
    squares = centre * centre
    phases = jnp.concatenate([depth * squares for depth in depths], axis=0)
    cosine, sine = turn_of_int(phases, 2 * cols_grid)
    cols_out[0] = cosine
    cols_out[1] = sine
    fetch.wait()
    coarse_count = cols_grid // LANES
    mids = LANES // FINE
    row_index = iota((rows_grid, LANES), 0)
    row_centre = row_index - rows_grid // 2
    row_squares = row_centre * row_centre
    for block in range(blocks):
        plane = lax.rem(codes[0, 0, block], limits[0, 0])
        planes[block] = plane
        depth = depths[0]
        for layer in range(1, layers):
            depth = jnp.where(plane >= layer, depths[layer], depth)
        u_pos = coords[0, 0, block, pl.ds(0, 1), :]
        v_pos = coords[0, 0, block, pl.ds(1, 1), :]
        half = cols_grid
        screen = ((depth * row_squares + half) & (2 * cols_grid - 1)) - half
        angle = wrap(row_index.astype(jnp.float32) * u_pos) + screen.astype(jnp.float32) * (
            1.0 / (2 * cols_grid)
        )
        cosine, sine = turn(wrap(angle))
        weight = jnp.where(block < limits[0, 1], vis_scale, 0.0)
        spot = pl.ds(block * LANES, LANES)
        u_tab[pl.ds(0, rows_grid), spot] = (cosine * weight).astype(jnp.bfloat16)
        u_tab[pl.ds(rows_grid, rows_grid), spot] = (sine * weight).astype(jnp.bfloat16)
        steps_wide = iota((coarse_count, LANES), 0).astype(jnp.float32)
        cosine, sine = turn(wrap(steps_wide * wrap(v_pos * float(LANES))))
        coarse_out[block, 0] = cosine
        coarse_out[block, 1] = sine
        steps_mid = iota((mids, LANES), 0).astype(jnp.float32)
        mid_cos, mid_sin = turn(wrap(steps_mid * wrap(v_pos * float(FINE))))
        steps_fine = iota((FINE, LANES), 0).astype(jnp.float32)
        fine_cos, fine_sin = turn(wrap(steps_fine * v_pos))
        for mid in range(mids):
            head_cos = mid_cos[mid : mid + 1]
            head_sin = mid_sin[mid : mid + 1]
            real = (head_cos * fine_cos - head_sin * fine_sin).astype(jnp.bfloat16)
            imag = (head_sin * fine_cos + head_cos * fine_sin).astype(jnp.bfloat16)
            upper = pl.ds(mid * FINE, FINE)
            lower = pl.ds(LANES + mid * FINE, FINE)
            kernels[block, upper, pl.ds(0, LANES)] = real
            kernels[block, upper, pl.ds(LANES, LANES)] = imag
            kernels[block, lower, pl.ds(0, LANES)] = -imag
            kernels[block, lower, pl.ds(LANES, LANES)] = real
    weights = jnp.dot(row_weights, u_tab[...], preferred_element_type=jnp.float32)
    for block in range(blocks):
        for part in range(2):
            rows_out[block, part] = weights[
                part * rows_grid : (part + 1) * rows_grid, block * LANES : (block + 1) * LANES
            ]


def degrid_kernel(
    dims, planes, local, passed, cols_tab, kernels, coarse, rows_tab, out, strips, layers_ref
):
    held, cols_grid, blocks, layers = dims
    wide = cols_grid // LANES
    lead = lax.axis_index("fy") % 2 == 1
    size = 2 * wide
    for index in range(held):
        spot = (index // (local.shape[1] * local.shape[2]),
                index // local.shape[2] % local.shape[1], index % local.shape[2])
        strips[pl.ds(index * size, size), :] = jnp.where(
            lead, local[spot].astype(jnp.float32), passed[spot].astype(jnp.float32)
        )
    for part in range(0, wide, 2):
        pair = []
        for col in (part, part + 1):
            real = strips[pl.ds(col, held, stride=2 * wide), :]
            imag = strips[pl.ds(wide + col, held, stride=2 * wide), :]
            pair.append((col, real, imag))
        rows = pl.ds(part * held, 2 * held)
        for layer in range(layers):
            turned_real, turned_imag = [], []
            for col, real, imag in pair:
                cols = pl.ds(col * LANES, LANES)
                cosine = cols_tab[0, pl.ds(layer, 1), cols]
                sine = cols_tab[1, pl.ds(layer, 1), cols]
                turned_real.append(real * cosine - imag * sine)
                turned_imag.append(real * sine + imag * cosine)
            layers_ref[layer, rows, pl.ds(0, LANES)] = jnp.concatenate(turned_real).astype(
                jnp.bfloat16
            )
            layers_ref[layer, rows, pl.ds(LANES, LANES)] = jnp.concatenate(turned_imag).astype(
                jnp.bfloat16
            )
    for block in range(blocks):
        sums = jnp.dot(layers_ref[planes[block]], kernels[block], preferred_element_type=jnp.float32)
        total_real = jnp.zeros((held, LANES), jnp.float32)
        total_imag = jnp.zeros((held, LANES), jnp.float32)
        for part in range(wide):
            sum_real = sums[part * held : (part + 1) * held, :LANES]
            sum_imag = sums[part * held : (part + 1) * held, LANES:]
            cosine = coarse[block, 0, pl.ds(part, 1), :]
            sine = coarse[block, 1, pl.ds(part, 1), :]
            total_real = total_real + (sum_real * cosine - sum_imag * sine)
            total_imag = total_imag + (sum_real * sine + sum_imag * cosine)
        row_cos = rows_tab[block, 0]
        row_sin = rows_tab[block, 1]
        vis_real = jnp.sum(row_cos * total_real - row_sin * total_imag, axis=0, keepdims=True)
        vis_imag = jnp.sum(row_cos * total_imag + row_sin * total_real, axis=0, keepdims=True)
        for part, value in enumerate((vis_real, vis_imag)):
            spot = (0, 0, block, pl.ds(part, 1), slice(None))
            out[spot] = value


def in_smem():
    return pl.BlockSpec(memory_space=pltpu.SMEM)


def in_vmem():
    return pl.BlockSpec(memory_space=pltpu.VMEM)


def kept(value):
    return pltpu.with_memory_space_constraint(value, pltpu.VMEM)


LIMIT = pltpu.CompilerParams(vmem_limit_bytes=16 << 20)
HOISTED = pltpu.CompilerParams(
    vmem_limit_bytes=16 << 20,
)


def per_device(
    sky_image, col_off, row_off, layer_counts, w_steps, live_blocks, block_codes, vis_coords
):
    rows_here, facet_cols = sky_image.shape
    num_cols = lax.axis_size("fx")
    num_rows = lax.axis_size("fy")
    half_z = num_cols // 2
    half_y = num_rows // 2
    total_cols = facet_cols * num_cols
    total_rows = rows_here * num_rows
    rows_grid = total_rows
    fine_cols = total_cols // LANES
    facet_rows = facet_cols // fine_cols
    wide = SG // LANES
    blocks = block_codes.shape[2]
    vis_count = vis_coords.shape[-1]
    layers = w_steps.shape[2]
    f32, bf16 = jnp.float32, jnp.bfloat16

    def exchange(value, flip, other_flip):
        pairs = [
            (i, i ^ (flip if i % 2 else other_flip)) for i in range(num_cols * num_rows)
        ]
        return lax.ppermute(value, ("fx", "fy"), pairs)

    near_flip = 2 * num_rows
    passed_sky = exchange(sky_image, 1, 1)
    arguments = (
        sky_image, vis_coords, col_off, row_off, w_steps, block_codes
    )
    own_sky, coords, *scalars = pl.pallas_call(
        load_kernel,
        name="load",
        out_shape=(
            pltpu.VMEM((rows_here, facet_rows, fine_cols), bf16),
            pltpu.VMEM(vis_coords.shape, f32),
            *(pltpu.SMEM(value.shape, value.dtype) for value in arguments[2:]),
        ),
        in_specs=[pl.BlockSpec(memory_space=pl.ANY)] * len(arguments),
        out_specs=(in_vmem(),) * 2 + (in_smem(),) * (len(arguments) - 2),
        scratch_shapes=[
            pltpu.VMEM(sky_image.shape, f32),
            pltpu.VMEM((rows_here * facet_cols // LANES, LANES), f32),
            pltpu.SemaphoreType.DMA((len(arguments),)),
        ],
        compiler_params=LIMIT,
    )(*(pltpu.with_memory_space_constraint(value, pltpu.HBM) for value in arguments))
    coords = kept(coords)
    col_off, row_off, w_steps, block_codes = (
        pltpu.with_memory_space_constraint(value, pltpu.SMEM) for value in scalars
    )
    chip_sky = pl.pallas_call(
        pack_kernel,
        name="pack",
        out_shape=pltpu.VMEM((2, rows_here, facet_rows, fine_cols), bf16),
        in_specs=[in_vmem()] * 2,
        out_specs=in_vmem(),
        scratch_shapes=[pltpu.VMEM((rows_here * facet_cols // LANES, LANES), f32)],
        compiler_params=LIMIT,
    )(kept(own_sky), kept(passed_sky))
    pieces = [chip_sky]
    for slot in range(1, half_z):
        pieces.append(exchange(chip_sky, 2 * slot * num_rows, near_flip))

    operands = [pieces[slot] for slot in slot_order(half_z)]

    first, twiddle, second = pl.pallas_call(
        functools.partial(
            column_tables_kernel,
            (half_z, facet_rows, fine_cols, total_cols, wide, 1.0 / math.sqrt(total_cols)),
        ),
        name="column_tables",
        out_shape=(
            pltpu.VMEM((half_z * facet_rows, 2 * LANES), bf16),
            pltpu.VMEM((2, fine_cols, 2 * LANES), f32),
            pltpu.VMEM((2 * wide, 2 * fine_cols), bf16),
        ),
        in_specs=[in_smem()],
        out_specs=(in_vmem(),) * 3,
        compiler_params=LIMIT,
    )(col_off)

    limits = jnp.where(
        lax.broadcasted_iota(jnp.int32, (1, LANES), 1) == 0, layer_counts, live_blocks
    )
    *tables, planes = pl.pallas_call(
        functools.partial(
            vis_tables_kernel,
            (
                half_y,
                rows_here,
                num_rows,
                rows_grid,
                SG,
                blocks,
                1.0 / math.sqrt(total_rows),
                1.0 / math.sqrt(rows_grid * SG),
            ),
        ),
        name="vis_tables",
        out_shape=(
            pltpu.VMEM((2, layers, SG), f32),
            pltpu.VMEM((blocks, 2 * LANES, 2 * vis_count), bf16),
            pltpu.VMEM((blocks, 2, wide, vis_count), f32),
            pltpu.VMEM((blocks, 2, rows_grid, vis_count), f32),
            pltpu.SMEM((blocks,), jnp.int32),
        ),
        in_specs=[in_smem()] * 3 + [in_vmem()] * 2,
        out_specs=(in_vmem(),) * 4 + (in_smem(),),
        scratch_shapes=[
            pltpu.SMEM((1, LANES), jnp.int32),
            pltpu.VMEM((2 * rows_grid, blocks * vis_count), bf16),
            pltpu.SemaphoreType.DMA,
        ],
        compiler_params=LIMIT,
    )(row_off, w_steps, block_codes, kept(limits), coords)

    band_shape = pltpu.VMEM((2, rows_here, 2 * wide, LANES), bf16)
    own_band, other_band = pl.pallas_call(
        functools.partial(band_kernel, (half_z, facet_rows, fine_cols, rows_here)),
        name="bands",
        out_shape=(band_shape, band_shape),
        in_specs=[in_smem()] + [in_vmem()] * (half_z + 3),
        out_specs=(in_vmem(),) * 2,
        compiler_params=LIMIT,
    )(col_off, *(kept(value) for value in (*operands, first, twiddle, second)))

    near, far = [own_band], []
    for slot in range(half_y):
        if slot:
            near.append(exchange(own_band, 2 * slot, near_flip))
        far.append(exchange(other_band, num_rows + 2 * slot, near_flip))
    near, far, tables = lax.optimization_barrier((near, far, tables))
    strips = [
        (one.astype(f32) + two.astype(f32)).astype(bf16) for one, two in zip(near, far)
    ]
    own_strips = jnp.stack(strips)
    passed_strips = exchange(own_strips, 1, 1)

    operands = [kept(value) for value in (own_strips, passed_strips, *tables)]
    return pl.pallas_call(
        functools.partial(degrid_kernel, (total_rows, SG, blocks, layers)),
        name="degrid",
        out_shape=jax.ShapeDtypeStruct(vis_coords.shape, f32),
        in_specs=[in_smem()] + [in_vmem()] * len(operands),
        out_specs=in_vmem(),
        scratch_shapes=[
            pltpu.VMEM((total_rows * 2 * wide, LANES), f32),
            pltpu.VMEM((layers, wide * total_rows, 2 * LANES), bf16),
        ],
        compiler_params=HOISTED,
    )(pltpu.with_memory_space_constraint(planes, pltpu.SMEM), *operands)


def solution(mesh):
    placed = (
        P("fy", "fx"),
        P(),
        P(),
        P("fx", "fy"),
        P("fx", "fy", None),
        P("fx", "fy"),
        P("fx", "fy", None),
        P("fx", "fy", None, None, None),
    )
    return jax.shard_map(
        per_device,
        mesh=mesh,
        in_specs=placed,
        out_specs=P("fx", "fy", None, None, None),
        check_vma=False,
    )
```

```python
import functools
import math

import jax
import jax.numpy as jnp
from jax import lax
from jax.experimental import pallas as pl
from jax.experimental.pallas import tpu as pltpu
from jax.sharding import PartitionSpec as P

SG = 1024
NSKY = 65536

LANES = 128
FINE = 16

COS_POLY = (
    0.9999999890590228,
    -19.73920449945383,
    64.93911745989081,
    -85.45013953079767,
    60.167630950263465,
    -25.967599245923743,
    6.52865815775625,
)
SIN_POLY = (
    6.283184916495428,
    -41.34158923268831,
    81.59994332977429,
    -76.61447253115396,
    41.34288235413569,
    -12.471243534350362,
)


def horner(coefficients, value):
    total = jnp.full_like(value, coefficients[-1])
    for coefficient in coefficients[-2::-1]:
        total = total * value + coefficient
    return total


def turn(fraction):
    square = fraction * fraction
    return horner(COS_POLY, square), fraction * horner(SIN_POLY, square)


def turn_of_int(count, modulus):
    half = modulus // 2
    centred = ((count + half) & (modulus - 1)) - half
    return turn(centred.astype(jnp.float32) * (1.0 / modulus))


def wrap(value):
    return value - jnp.round(value)


def iota(shape, axis):
    return lax.broadcasted_iota(jnp.int32, shape, axis)


def settle(flat, split, target):
    rows, pieces, width = target.shape
    parts = width // LANES
    for piece in range(pieces):
        for part in range(parts):
            split[pl.ds(part * rows * pieces + piece, rows, stride=pieces), :] = flat[
                :, pl.ds((piece * parts + part) * LANES, LANES)
            ]
    for row in range(rows):
        for part in range(parts):
            here = pl.ds((part * rows + row) * pieces, pieces)
            target[row, :, pl.ds(part * LANES, LANES)] = split[here, :].astype(jnp.bfloat16)


def pack_kernel(own, passed, out, split):
    out[0] = own[...]
    settle(passed, split, out.at[1])


def load_kernel(*refs):
    count = (len(refs) - 3) // 2
    sources, (sky_out, *targets) = refs[:count], refs[count : 2 * count]
    landed, split, semaphores = refs[2 * count :]
    copies = [
        pltpu.make_async_copy(source, target, semaphores.at[index])
        for index, (source, target) in enumerate(zip(sources, [landed, *targets]))
    ]
    for copy in copies:
        copy.start()
    copies[0].wait()
    settle(landed, split, sky_out)
    for copy in copies[1:]:
        copy.wait()


def column_tables_kernel(dims, col_off, first, twiddle, second):
    half_z, facet_rows, fine_cols, total_cols, wide, scale = dims
    here = lax.axis_index("fx")
    for slot in range(half_z):
        row = facet_rows * (here ^ (2 * slot)) + iota((facet_rows, LANES), 0)
        cosine, sine = turn_of_int(row * iota((facet_rows, LANES), 1), LANES)
        rows = pl.ds(slot * facet_rows, facet_rows)
        first[rows, pl.ds(0, LANES)] = cosine.astype(jnp.bfloat16)
        first[rows, pl.ds(LANES, LANES)] = (-sine).astype(jnp.bfloat16)
    for target in range(2):
        offset = col_off[here ^ target]
        residue = iota((fine_cols, LANES), 1)
        step = (residue - offset) & (LANES - 1)
        cosine, sine = turn_of_int(iota((fine_cols, LANES), 0) * (offset + step), total_cols)
        cols = pl.ds(target * LANES, LANES)
        twiddle[0, :, cols] = cosine * scale
        twiddle[1, :, cols] = sine * (-scale)
    cosine, sine = turn_of_int(iota((wide, fine_cols), 0) * iota((wide, fine_cols), 1), fine_cols)
    second[pl.ds(0, wide), pl.ds(0, fine_cols)] = cosine.astype(jnp.bfloat16)
    second[pl.ds(0, wide), pl.ds(fine_cols, fine_cols)] = sine.astype(jnp.bfloat16)
    second[pl.ds(wide, wide), pl.ds(0, fine_cols)] = (-sine).astype(jnp.bfloat16)
    second[pl.ds(wide, wide), pl.ds(fine_cols, fine_cols)] = cosine.astype(jnp.bfloat16)


def slot_order(half_z):
    return [*range(min(2, half_z)), *range(half_z - 1, 1, -1)]


def band_kernel(dims, col_off, *refs):
    half_z, facet_rows, fine_cols, rows_here = dims
    here = lax.axis_index("fx")
    shifts = [(-col_off[here ^ target]) & (LANES - 1) for target in range(2)]
    pieces = [refs[place] for place in slot_order(half_z)]
    first, twiddle, second, own_out, other_out = refs[half_z:]
    twist_real = twiddle[0]
    twist_imag = twiddle[1]
    for held in range(2):
        stacked = jnp.concatenate(
            [
                jnp.concatenate([piece[held, row] for piece in pieces], axis=0)
                for row in range(rows_here)
            ],
            axis=1,
        )
        spread = lax.dot_general(
            stacked, first[...], (((0,), (0,)), ((), ())), preferred_element_type=jnp.float32
        )
        for row in range(rows_here):
            part = spread[row * fine_cols : (row + 1) * fine_cols]
            part_real = jnp.concatenate([part[:, :LANES]] * 2, axis=1)
            part_imag = jnp.concatenate([part[:, LANES:]] * 2, axis=1)
            turned = jnp.concatenate(
                [
                    part_real * twist_real - part_imag * twist_imag,
                    part_real * twist_imag + part_imag * twist_real,
                ],
                axis=0,
            ).astype(jnp.bfloat16)
            bands = jnp.dot(second[...], turned, preferred_element_type=jnp.float32)
            for target, out in enumerate((own_out, other_out)):
                band = bands[:, target * LANES : (target + 1) * LANES]
                out[held, row] = pltpu.roll(band, shifts[target], 1).astype(jnp.bfloat16)


def vis_tables_kernel(
    dims, row_off, steps, codes, limits_in, coords,
    cols_out, kernels, coarse_out, rows_out, planes, limits, u_tab, semaphore,
):
    half_y, rows_here, num_rows, rows_grid, cols_grid, blocks, row_scale, vis_scale = dims
    here = lax.axis_index("fy")
    fetch = pltpu.make_async_copy(limits_in, limits, semaphore)
    fetch.start()
    shape = (2 * rows_grid, 2 * rows_grid)
    order = iota(shape, 0)
    imag_out = order // rows_grid
    slot = (order // (2 * rows_here)) % half_y
    owner = ((here | 1) ^ (2 * slot)) - (order // rows_here) % 2
    sky_row = owner * (NSKY // num_rows) + order % rows_here
    column = iota(shape, 1)
    imag_in = column // rows_grid
    wave = row_off[here] + column % rows_grid
    cosine, sine = turn_of_int(sky_row * (wave & (NSKY - 1)), NSKY)
    cross = jnp.where(imag_out == 0, sine, -sine)
    row_weights = (jnp.where(imag_in == imag_out, cosine, cross) * row_scale).astype(jnp.bfloat16)
    layers = steps.shape[2]
    depths = []
    depth = steps[0, 0, 0]
    for layer in range(layers):
        if layer:
            depth = depth + steps[0, 0, layer]
        depths.append(depth)
    centre = iota((1, cols_grid), 1) - cols_grid // 2
    squares = centre * centre
    phases = jnp.concatenate([depth * squares for depth in depths], axis=0)
    cosine, sine = turn_of_int(phases, 2 * cols_grid)
    for layer in range(layers):
        for part in range(cols_grid // LANES):
            spot = (slice(layer, layer + 1), slice(part * LANES, (part + 1) * LANES))
            for side, value in enumerate((cosine, sine)):
                cols_out[side, layer, part] = jnp.broadcast_to(
                    value[spot], (rows_grid, LANES)
                ).astype(jnp.bfloat16)
    fetch.wait()
    coarse_count = cols_grid // LANES
    mids = LANES // FINE
    row_index = iota((rows_grid, LANES), 0)
    row_centre = row_index - rows_grid // 2
    row_squares = row_centre * row_centre
    for block in range(blocks):
        plane = lax.rem(codes[0, 0, block], limits[0, 0])
        planes[block] = plane
        depth = depths[0]
        for layer in range(1, layers):
            depth = jnp.where(plane >= layer, depths[layer], depth)
        u_pos = coords[0, 0, block, pl.ds(0, 1), :]
        v_pos = coords[0, 0, block, pl.ds(1, 1), :]
        half = cols_grid
        screen = ((depth * row_squares + half) & (2 * cols_grid - 1)) - half
        angle = wrap(row_index.astype(jnp.float32) * u_pos) + screen.astype(jnp.float32) * (
            1.0 / (2 * cols_grid)
        )
        cosine, sine = turn(wrap(angle))
        weight = jnp.where(block < limits[0, 1], vis_scale, 0.0)
        spot = pl.ds(block * LANES, LANES)
        u_tab[pl.ds(0, rows_grid), spot] = (cosine * weight).astype(jnp.bfloat16)
        u_tab[pl.ds(rows_grid, rows_grid), spot] = (sine * weight).astype(jnp.bfloat16)
        steps_wide = iota((coarse_count, LANES), 0).astype(jnp.float32)
        cosine, sine = turn(wrap(steps_wide * wrap(v_pos * float(LANES))))
        coarse_out[block, 0] = cosine
        coarse_out[block, 1] = sine
        steps_mid = iota((mids, LANES), 0).astype(jnp.float32)
        mid_cos, mid_sin = turn(wrap(steps_mid * wrap(v_pos * float(FINE))))
        steps_fine = iota((FINE, LANES), 0).astype(jnp.float32)
        fine_cos, fine_sin = turn(wrap(steps_fine * v_pos))
        for mid in range(mids):
            head_cos = mid_cos[mid : mid + 1]
            head_sin = mid_sin[mid : mid + 1]
            real = (head_cos * fine_cos - head_sin * fine_sin).astype(jnp.bfloat16)
            imag = (head_sin * fine_cos + head_cos * fine_sin).astype(jnp.bfloat16)
            upper = pl.ds(mid * FINE, FINE)
            lower = pl.ds(LANES + mid * FINE, FINE)
            kernels[block, upper, pl.ds(0, LANES)] = real
            kernels[block, upper, pl.ds(LANES, LANES)] = imag
            kernels[block, lower, pl.ds(0, LANES)] = -imag
            kernels[block, lower, pl.ds(LANES, LANES)] = real
    weights = jnp.dot(row_weights, u_tab[...], preferred_element_type=jnp.float32)
    for block in range(blocks):
        for part in range(2):
            rows_out[block, part] = weights[
                part * rows_grid : (part + 1) * rows_grid, block * LANES : (block + 1) * LANES
            ]


def degrid_kernel(
    dims, planes, local, passed, cols_tab, kernels, coarse, rows_tab, out, strips, layers_ref
):
    held, cols_grid, blocks, layers = dims
    wide = cols_grid // LANES
    lead = lax.axis_index("fy") % 2 == 1
    size = 2 * wide
    for index in range(held):
        spot = (index // (local.shape[1] * local.shape[2]),
                index // local.shape[2] % local.shape[1], index % local.shape[2])
        strips[pl.ds(index * size, size), :] = jnp.where(
            lead, local[spot].astype(jnp.float32), passed[spot].astype(jnp.float32)
        )
    for part in range(wide):
        real = strips[pl.ds(part, held, stride=2 * wide), :].astype(jnp.bfloat16)
        imag = strips[pl.ds(wide + part, held, stride=2 * wide), :].astype(jnp.bfloat16)
        rows = pl.ds(part * held, held)
        for layer in range(layers):
            cosine = cols_tab[0, layer, part]
            sine = cols_tab[1, layer, part]
            layers_ref[layer, rows, pl.ds(0, LANES)] = real * cosine - imag * sine
            layers_ref[layer, rows, pl.ds(LANES, LANES)] = real * sine + imag * cosine
    for block in range(blocks):
        sums = jnp.dot(layers_ref[planes[block]], kernels[block], preferred_element_type=jnp.float32)
        total_real = jnp.zeros((held, LANES), jnp.float32)
        total_imag = jnp.zeros((held, LANES), jnp.float32)
        for part in range(wide):
            sum_real = sums[part * held : (part + 1) * held, :LANES]
            sum_imag = sums[part * held : (part + 1) * held, LANES:]
            cosine = coarse[block, 0, pl.ds(part, 1), :]
            sine = coarse[block, 1, pl.ds(part, 1), :]
            total_real = total_real + (sum_real * cosine - sum_imag * sine)
            total_imag = total_imag + (sum_real * sine + sum_imag * cosine)
        row_cos = rows_tab[block, 0]
        row_sin = rows_tab[block, 1]
        vis_real = jnp.sum(row_cos * total_real - row_sin * total_imag, axis=0, keepdims=True)
        vis_imag = jnp.sum(row_cos * total_imag + row_sin * total_real, axis=0, keepdims=True)
        for part, value in enumerate((vis_real, vis_imag)):
            spot = (0, 0, block, pl.ds(part, 1), slice(None))
            out[spot] = value


def in_smem():
    return pl.BlockSpec(memory_space=pltpu.SMEM)


def in_vmem():
    return pl.BlockSpec(memory_space=pltpu.VMEM)


def kept(value):
    return pltpu.with_memory_space_constraint(value, pltpu.VMEM)


LIMIT = pltpu.CompilerParams(vmem_limit_bytes=16 << 20)


def per_device(
    sky_image, col_off, row_off, layer_counts, w_steps, live_blocks, block_codes, vis_coords
):
    rows_here, facet_cols = sky_image.shape
    num_cols = lax.axis_size("fx")
    num_rows = lax.axis_size("fy")
    half_z = num_cols // 2
    half_y = num_rows // 2
    total_cols = facet_cols * num_cols
    total_rows = rows_here * num_rows
    rows_grid = total_rows
    fine_cols = total_cols // LANES
    facet_rows = facet_cols // fine_cols
    wide = SG // LANES
    blocks = block_codes.shape[2]
    vis_count = vis_coords.shape[-1]
    layers = w_steps.shape[2]
    f32, bf16 = jnp.float32, jnp.bfloat16

    def exchange(value, flip, other_flip):
        pairs = [
            (i, i ^ (flip if i % 2 else other_flip)) for i in range(num_cols * num_rows)
        ]
        return lax.ppermute(value, ("fx", "fy"), pairs)

    near_flip = 2 * num_rows
    passed_sky = exchange(sky_image, 1, 1)
    arguments = (
        sky_image, vis_coords, col_off, row_off, w_steps, block_codes
    )
    own_sky, coords, *scalars = pl.pallas_call(
        load_kernel,
        name="load",
        out_shape=(
            pltpu.VMEM((rows_here, facet_rows, fine_cols), bf16),
            pltpu.VMEM(vis_coords.shape, f32),
            *(pltpu.SMEM(value.shape, value.dtype) for value in arguments[2:]),
        ),
        in_specs=[pl.BlockSpec(memory_space=pl.ANY)] * len(arguments),
        out_specs=(in_vmem(),) * 2 + (in_smem(),) * (len(arguments) - 2),
        scratch_shapes=[
            pltpu.VMEM(sky_image.shape, f32),
            pltpu.VMEM((rows_here * facet_cols // LANES, LANES), f32),
            pltpu.SemaphoreType.DMA((len(arguments),)),
        ],
        compiler_params=LIMIT,
    )(*(pltpu.with_memory_space_constraint(value, pltpu.HBM) for value in arguments))
    coords = kept(coords)
    col_off, row_off, w_steps, block_codes = (
        pltpu.with_memory_space_constraint(value, pltpu.SMEM) for value in scalars
    )
    chip_sky = pl.pallas_call(
        pack_kernel,
        name="pack",
        out_shape=pltpu.VMEM((2, rows_here, facet_rows, fine_cols), bf16),
        in_specs=[in_vmem()] * 2,
        out_specs=in_vmem(),
        scratch_shapes=[pltpu.VMEM((rows_here * facet_cols // LANES, LANES), f32)],
        compiler_params=LIMIT,
    )(kept(own_sky), kept(passed_sky))
    pieces = [chip_sky]
    for slot in range(1, half_z):
        pieces.append(exchange(chip_sky, 2 * slot * num_rows, near_flip))

    operands = [pieces[slot] for slot in slot_order(half_z)]

    first, twiddle, second = pl.pallas_call(
        functools.partial(
            column_tables_kernel,
            (half_z, facet_rows, fine_cols, total_cols, wide, 1.0 / math.sqrt(total_cols)),
        ),
        name="column_tables",
        out_shape=(
            pltpu.VMEM((half_z * facet_rows, 2 * LANES), bf16),
            pltpu.VMEM((2, fine_cols, 2 * LANES), f32),
            pltpu.VMEM((2 * wide, 2 * fine_cols), bf16),
        ),
        in_specs=[in_smem()],
        out_specs=(in_vmem(),) * 3,
        compiler_params=LIMIT,
    )(col_off)

    limits = jnp.where(
        lax.broadcasted_iota(jnp.int32, (1, LANES), 1) == 0, layer_counts, live_blocks
    )
    *tables, planes = pl.pallas_call(
        functools.partial(
            vis_tables_kernel,
            (
                half_y,
                rows_here,
                num_rows,
                rows_grid,
                SG,
                blocks,
                1.0 / math.sqrt(total_rows),
                1.0 / math.sqrt(rows_grid * SG),
            ),
        ),
        name="vis_tables",
        out_shape=(
            pltpu.VMEM((2, layers, wide, rows_grid, LANES), bf16),
            pltpu.VMEM((blocks, 2 * LANES, 2 * vis_count), bf16),
            pltpu.VMEM((blocks, 2, wide, vis_count), f32),
            pltpu.VMEM((blocks, 2, rows_grid, vis_count), f32),
            pltpu.SMEM((blocks,), jnp.int32),
        ),
        in_specs=[in_smem()] * 3 + [in_vmem()] * 2,
        out_specs=(in_vmem(),) * 4 + (in_smem(),),
        scratch_shapes=[
            pltpu.SMEM((1, LANES), jnp.int32),
            pltpu.VMEM((2 * rows_grid, blocks * vis_count), bf16),
            pltpu.SemaphoreType.DMA,
        ],
        compiler_params=LIMIT,
    )(row_off, w_steps, block_codes, kept(limits), coords)

    band_shape = pltpu.VMEM((2, rows_here, 2 * wide, LANES), bf16)
    own_band, other_band = pl.pallas_call(
        functools.partial(band_kernel, (half_z, facet_rows, fine_cols, rows_here)),
        name="bands",
        out_shape=(band_shape, band_shape),
        in_specs=[in_smem()] + [in_vmem()] * (half_z + 3),
        out_specs=(in_vmem(),) * 2,
        compiler_params=LIMIT,
    )(col_off, *(kept(value) for value in (*operands, first, twiddle, second)))

    near, far = [own_band], []
    for slot in range(half_y):
        if slot:
            near.append(exchange(own_band, 2 * slot, near_flip))
        far.append(exchange(other_band, num_rows + 2 * slot, near_flip))
    near, far, tables = lax.optimization_barrier((near, far, tables))
    strips = [
        (one.astype(f32) + two.astype(f32)).astype(bf16) for one, two in zip(near, far)
    ]
    own_strips = jnp.stack(strips)
    passed_strips = exchange(own_strips, 1, 1)

    operands = [kept(value) for value in (own_strips, passed_strips, *tables)]
    return pl.pallas_call(
        functools.partial(degrid_kernel, (total_rows, SG, blocks, layers)),
        name="degrid",
        out_shape=jax.ShapeDtypeStruct(vis_coords.shape, f32),
        in_specs=[in_smem()] + [in_vmem()] * len(operands),
        out_specs=in_vmem(),
        scratch_shapes=[
            pltpu.VMEM((total_rows * 2 * wide, LANES), f32),
            pltpu.VMEM((layers, wide * total_rows, 2 * LANES), bf16),
        ],
        compiler_params=LIMIT,
    )(pltpu.with_memory_space_constraint(planes, pltpu.SMEM), *operands)


def solution(mesh):
    placed = (
        P("fy", "fx"),
        P(),
        P(),
        P("fx", "fy"),
        P("fx", "fy", None),
        P("fx", "fy"),
        P("fx", "fy", None),
        P("fx", "fy", None, None, None),
    )
    return jax.shard_map(
        per_device,
        mesh=mesh,
        in_specs=placed,
        out_specs=P("fx", "fy", None, None, None),
        check_vma=False,
    )
```
